32 devices in a mesh: ctx: 8 (over z, y), tp: 4 (over x, core).
Axes of the slice: x: 2, y: 2, z: 4, core: 2. Of those that a mesh axis runs over, the one named last changes fastest.
Arguments:
- layer_inputs: bfloat16 [1536, 2048], P('ctx', 'tp'), may hold values from -6 to 6
- states: float32 [1536, 2048], P('ctx', 'tp'), may hold values from -0.7 to 0.7
- cotangent: float32 [1536, 2048], P('ctx', 'tp'), may hold values from -0.009765625 to 0.009765625
- block_weights: float32 [32, 64, 64], P('tp'), may hold values from -1 to 1
Outputs:
- grad_proj: float32 [2048, 2048], P(('ctx', 'tp'))
The draws below stay inside these ranges and needn't reach their ends.
All inputs are finite; a program needn't handle non-finite values.
Results may differ from the reference program's by a relative error of at most 0.0029.
Values may be sent and summed in bfloat16 or wider, within the bound.
A program may use at most 64 MiB of HBM per device.

```python
from functools import partial
import jax
import jax.numpy as jnp
from jax import lax

D = 2048
HEADS = 32
HEAD = 64
HID = 2048
SEQUENCE_TOKENS = 1536


def head_plan(key):
    order = jax.random.permutation(jax.random.fold_in(key, 11), HEADS)
    slow_heads = order < HEADS // 2
    return slow_heads


def draw_block_weights(key, part):
    slow_heads = head_plan(key)
    normals = jax.random.normal(jax.random.fold_in(key, 12), (HEADS, HEAD, HEAD), jnp.float32)
    factors = jnp.linalg.qr(normals)
    rotations = factors[0]
    decay_rates = jax.random.uniform(jax.random.fold_in(key, 13), (HEADS,), jnp.float32, 0.96, 0.985)
    head_scale = jnp.where(slow_heads, 1.0, decay_rates)
    return rotations * head_scale[:, None, None]


def draw_states(key, part):
    slow_heads = head_plan(key)
    shape = (SEQUENCE_TOKENS, HEADS * HEAD)
    head_rates = jax.random.uniform(jax.random.fold_in(key, 18), (HEADS,), jnp.float32, 0.5, 1.2)
    dense_level = jnp.sqrt(3.0 * 0.15 * head_rates / SEQUENCE_TOKENS)
    peak_level = jnp.sqrt(0.85 * head_rates / (SEQUENCE_TOKENS * 0.0125 * 0.5833))
    slow_units = jnp.repeat(slow_heads, HEAD)
    dense_amplitude = jnp.repeat(jnp.where(slow_heads, dense_level, 0.15), HEAD)
    dense_part = jax.random.uniform(jax.random.fold_in(key, 14), shape, jnp.float32, -1.0, 1.0) * dense_amplitude[None, :]
    hit_mask = jax.random.bernoulli(jax.random.fold_in(key, 19), 0.0125, shape)
    magnitudes = jax.random.uniform(jax.random.fold_in(key, 20), shape, jnp.float32, 0.5, 1.0) * jnp.repeat(peak_level, HEAD)[None, :]
    magnitudes = jnp.minimum(magnitudes, 0.65)
    quiet_sign = jnp.where(jax.random.bernoulli(jax.random.fold_in(key, 21), 0.5, shape), 1.0, -1.0)
    quiet_part = jnp.where(slow_units[None, :] & hit_mask, quiet_sign * magnitudes, dense_part)
    spike_rows = jax.random.randint(jax.random.fold_in(key, 15), (3,), 0, SEQUENCE_TOKENS)
    token_positions = jnp.arange(SEQUENCE_TOKENS)
    spiking_active = jnp.any(token_positions[:, None] == spike_rows[None, :], axis=1)
    levels = jax.random.uniform(jax.random.fold_in(key, 16), shape, jnp.float32, 0.45, 0.6)
    polarity = jnp.where(jax.random.bernoulli(jax.random.fold_in(key, 17), 0.5, shape), 1.0, -1.0)
    return jnp.where(spiking_active[:, None], levels * polarity, quiet_part)


def shard_levels(rng, extent, split, low, top_value):
    def one(axis_at, blocks):
        steps = jax.random.uniform(jax.random.fold_in(jax.random.fold_in(rng, 6), axis_at), (blocks,), jnp.float32, low / len(split), top_value / len(split))
        return jnp.repeat(jnp.exp(steps), extent[axis_at] // blocks).reshape((-1,) + (1,) * (len(extent) - axis_at - 1))

    level = one(*split[0])
    for cut in split[1:]:
        level = level * one(*cut)
    return level


def gaussian(own_key, dims, spread, limit, shards=(), dtype=jnp.bfloat16):
    gain = shard_levels(own_key, dims, shards, -0.22, 0.18) if shards else 1.0
    entries = jax.random.normal(own_key, dims, jnp.float32) * spread * gain
    return jnp.minimum(jnp.maximum(entries, -limit), limit).astype(dtype)


def setup_inputs(seed: int = 0) -> dict:
    arg_keys = jax.random.split(jax.random.key(seed), 5)
    return {
        "layer_inputs": gaussian(arg_keys[0], (SEQUENCE_TOKENS, D), 1.0, 6.0, ((0, 8), (1, 4))),
        "states": draw_states(jax.random.fold_in(arg_keys[4], 71), 0),
        "cotangent": gaussian(arg_keys[2], (SEQUENCE_TOKENS, HID), (1.0 / SEQUENCE_TOKENS), 0.009765625, ((0, 8), (1, 4)), jnp.float32),
        "block_weights": draw_block_weights(jax.random.fold_in(arg_keys[4], 71), 0),
    }


def step_back(block_weights, subsequent_step, pieces):
    slopes, upstream = pieces
    pulled = jnp.einsum('kji,kj->ki', block_weights, subsequent_step, precision=lax.Precision.HIGHEST)
    current = slopes * (upstream + pulled)
    return (current, current)

def reference(layer_inputs, states, cotangent, block_weights):
    slopes = (1.0 - states * states).reshape(SEQUENCE_TOKENS, HEADS, HEAD)
    upstream = cotangent.reshape(SEQUENCE_TOKENS, HEADS, HEAD)
    initial = jnp.zeros((HEADS, HEAD), jnp.float32)
    remaining_part, adjoints = lax.scan(partial(step_back, block_weights), initial, (slopes, upstream), reverse=True)
    adjoint_bf = adjoints.reshape(SEQUENCE_TOKENS, HEADS * HEAD).astype(jnp.bfloat16)
    return jnp.dot(jnp.transpose(layer_inputs).astype(jnp.float32), adjoint_bf.astype(jnp.float32), preferred_element_type=jnp.float32)
```

```python
import functools
import jax
import jax.numpy as jnp
from jax import lax
from jax.experimental import pallas as pl
from jax.experimental.pallas import tpu as pltpu
from jax.sharding import PartitionSpec as P

MESH = pl.DeviceIdType.MESH
CHUNKS = 8
F32 = jnp.float32
BF16 = jnp.bfloat16


def halves(value):
    high = value.astype(BF16)
    low = (value - high.astype(F32)).astype(BF16)
    return high, low


def dot(left, right):
    return jnp.dot(left, right, preferred_element_type=F32)


def dot3(left, right_high, right_low):
    high, low = halves(left)
    return dot(high, right_high) + (dot(low, right_high) + dot(high, right_low))


def block_mask(width, head):
    rows = lax.broadcasted_iota(jnp.int32, (width, width), 0) // head
    cols = lax.broadcasted_iota(jnp.int32, (width, width), 1) // head
    return rows == cols


def recurrence(states_ref, cot_ref, weights_ref, adj_ref,
               maps, offsets, suffix, suffix_vec, spread_e, full, e_in, e_out,
               send_sem, recv_sem):
    n = lax.axis_size("ctx")
    me = lax.axis_index("ctx")
    tokens, units = states_ref.shape
    head = weights_ref.shape[0]
    length = tokens // CHUNKS
    width = min(256, units)
    groups = units // width
    tile = width // head

    barrier = pltpu.get_barrier_semaphore()
    pl.semaphore_signal(barrier, inc=1, device_id={"ctx": lax.rem(me + 1, n)}, device_id_type=MESH)
    pl.semaphore_signal(barrier, inc=1, device_id={"ctx": lax.rem(me + n - 1, n)}, device_id_type=MESH)

    mask = block_mask(width, head)

    def spread(rows):
        return halves(jnp.where(mask, jnp.concatenate([rows] * tile, axis=0), 0.0))

    last = length - 1
    weights = [spread(weights_ref[:, g * width:(g + 1) * width]) for g in range(groups)]

    def token_rows(ref, t):
        return jnp.concatenate([ref[k, pl.ds(t, 1), :] for k in range(CHUNKS)], axis=0)

    def slopes_at(t):
        h = token_rows(states_ref_view, t)
        return 1.0 - h * h

    states_ref_view = states_ref.reshape(CHUNKS, length, units)
    cot_ref_view = cot_ref.reshape(CHUNKS, length, units)
    full_view = full.reshape(CHUNKS, length, units)

    s_last = slopes_at(last)
    offsets[last] = s_last * token_rows(cot_ref_view, last)
    for k in range(CHUNKS):
        maps[last, k * head:(k + 1) * head, :] = weights_ref[...] * s_last[k:k + 1, :]

    def step(i, carry):
        t = last - 1 - i
        s = slopes_at(t)
        c = token_rows(cot_ref_view, t)
        for g in range(groups):
            lanes = slice(g * width, (g + 1) * width)
            high, low = weights[g]
            v = offsets[t + 1, :, lanes]
            offsets[t, :, lanes] = s[:, lanes] * (c[:, lanes] + dot3(v, high, low))
            for k in range(CHUNKS):
                rows = slice(k * head, (k + 1) * head)
                y = dot3(maps[t + 1, rows, lanes], high, low)
                maps[t, rows, lanes] = y * s[k:k + 1, lanes]
        return carry

    lax.fori_loop(0, last, step, 0)

    for g in range(groups):
        lanes = slice(g * width, (g + 1) * width)
        top = (CHUNKS - 1) * head
        running = maps[0, top:top + head, lanes]
        vec = offsets[0, CHUNKS - 1:CHUNKS, lanes]
        suffix[top:top + head, lanes] = running
        suffix_vec[CHUNKS - 1:CHUNKS, lanes] = vec
        for k in range(CHUNKS - 2, -1, -1):
            rows = slice(k * head, (k + 1) * head)
            high, low = spread(maps[0, rows, lanes])
            running = dot3(running, high, low)
            vec = dot3(jnp.broadcast_to(vec, (8, width)), high, low)[0:1] + offsets[0, k:k + 1, lanes]
            suffix[rows, lanes] = running
            suffix_vec[k:k + 1, lanes] = vec

    ones = mask.astype(F32).astype(BF16)
    pick = (lax.broadcasted_iota(jnp.int32, (head, width), 1) % head
            == lax.broadcasted_iota(jnp.int32, (head, width), 0))

    def replicate(row):
        high, low = halves(jnp.where(pick, jnp.broadcast_to(row, (head, width)), 0.0))
        return dot(high, ones) + dot(low, ones)

    pl.semaphore_wait(barrier, 2)
    copy = pltpu.make_async_remote_copy(
        src_ref=e_out, dst_ref=e_in, send_sem=send_sem, recv_sem=recv_sem,
        device_id={"ctx": lax.max(me - 1, 0)}, device_id_type=MESH)

    @pl.when(me == n - 1)
    def _():
        e_in[...] = jnp.zeros_like(e_in)

    @pl.when(me < n - 1)
    def _():
        copy.wait_recv()

    spreads = []
    for g in range(groups):
        lanes = slice(g * width, (g + 1) * width)
        e = replicate(e_in[:, lanes])
        spreads.append(e)
        e_out[:, lanes] = suffix_vec[0:1, lanes] + jnp.sum(
            e * suffix[0:head, lanes], axis=0, keepdims=True)

    @pl.when(me > 0)
    def _():
        copy.start()

    for g in range(groups):
        lanes = slice(g * width, (g + 1) * width)
        e = spreads[g]
        top = (CHUNKS - 1) * head
        spread_e[top:top + head, lanes] = e
        for k in range(1, CHUNKS):
            start = suffix_vec[k:k + 1, lanes] + jnp.sum(
                e * suffix[k * head:(k + 1) * head, lanes], axis=0, keepdims=True)
            spread_e[(k - 1) * head:k * head, lanes] = replicate(start)

    for k in range(CHUNKS):
        rows = slice(k * head, (k + 1) * head)

        def solve(t, carry):
            value = offsets[t, k:k + 1, :] + jnp.sum(
                maps[t, rows, :] * spread_e[rows, :], axis=0, keepdims=True)
            full_view[k, pl.ds(t, 1), :] = value
            return carry

        lax.fori_loop(0, length, solve, 0, unroll=4)
    adj_ref[...] = full[...].astype(BF16)

    @pl.when(me > 0)
    def _():
        copy.wait_send()


def on_device(layer_inputs, states, cotangent, block_weights):
    tokens, units = states.shape
    heads, head, _ = block_weights.shape
    length = tokens // CHUNKS
    flat = jnp.transpose(block_weights, (1, 0, 2)).reshape(head, units)
    vmem = pl.BlockSpec(memory_space=pltpu.VMEM)
    adj = pl.pallas_call(
        recurrence,
        out_shape=jax.ShapeDtypeStruct((tokens, units), BF16),
        in_specs=[vmem] * 3,
        out_specs=vmem,
        scratch_shapes=[
            pltpu.VMEM((length, CHUNKS * head, units), F32),
            pltpu.VMEM((length, CHUNKS, units), F32),
            pltpu.VMEM((CHUNKS * head, units), F32),
            pltpu.VMEM((CHUNKS, units), F32),
            pltpu.VMEM((CHUNKS * head, units), F32),
            pltpu.VMEM((tokens, units), F32),
            pltpu.VMEM((1, units), F32),
            pltpu.VMEM((1, units), F32),
            pltpu.SemaphoreType.DMA,
            pltpu.SemaphoreType.DMA,
        ],
        compiler_params=pltpu.CompilerParams(
            collective_id=0, has_side_effects=True, vmem_limit_bytes=48 * 1024 * 1024),
    )(states, cotangent, flat)
    wide = lax.all_gather(layer_inputs, "tp", axis=1, tiled=True)
    mine = lax.all_to_all(wide, "ctx", split_axis=1, concat_axis=0, tiled=True)
    every = lax.all_gather(adj, "ctx", axis=0, tiled=True)
    block = lax.dot_general(mine, every, (((0,), (0,)), ((), ())), preferred_element_type=F32)
    return lax.all_to_all(block, "tp", split_axis=0, concat_axis=1, tiled=True)


def solution(mesh):
    in_specs = (P("ctx", "tp"), P("ctx", "tp"), P("ctx", "tp"), P("tp", None, None))
    out_specs = P(("ctx", "tp"), None)
    return jax.shard_map(
        on_device, mesh=mesh, in_specs=in_specs, out_specs=out_specs, check_vma=False
    )
```

```python
import jax
import jax.numpy as jnp
from jax import lax
from jax.experimental import pallas as pl
from jax.experimental.pallas import tpu as pltpu
from jax.sharding import PartitionSpec as P

MESH = pl.DeviceIdType.MESH
CHUNKS = 8
PAD = 16
F32 = jnp.float32
BF16 = jnp.bfloat16


def halves(value):
    high = value.astype(BF16)
    low = (value - high.astype(F32)).astype(BF16)
    return high, low


def dot(left, right):
    return jnp.dot(left, right, preferred_element_type=F32)


def left_terms(value):
    high, low = halves(value)
    return jnp.concatenate([high, low, high], axis=1)


def right_terms(value):
    high, low = halves(value)
    return jnp.concatenate([high, high, low], axis=0)


def recurrence(states_ref, cot_ref, weights_ref, pieces_ref, adj_ref, mine_ref,
               maps, weights, suffix, suffix_vec, spread_e, full, e_in, e_out,
               send_sem, recv_sem, local_sem, piece_send, piece_recv):
    n = lax.axis_size("ctx")
    ranks = lax.axis_size("tp")
    me = lax.axis_index("ctx")
    rank = lax.axis_index("tp")
    tokens, units = states_ref.shape
    head = weights_ref.shape[0]
    length = tokens // CHUNKS
    width = min(256, units)
    groups = units // width
    tile = width // head
    rows_all = CHUNKS * head
    pieces = pieces_ref.shape[0]
    last = length - 1

    barrier = pltpu.get_barrier_semaphore()
    pl.semaphore_signal(barrier, inc=1, device_id={"ctx": lax.rem(me + 1, n)}, device_id_type=MESH)
    pl.semaphore_signal(barrier, inc=1, device_id={"ctx": lax.rem(me + n - 1, n)}, device_id_type=MESH)
    source_rank = me // pieces
    own = source_rank == rank
    for c in range(n):
        @pl.when(jnp.logical_not(jnp.logical_and(own, me == c)))
        def _():
            pl.semaphore_signal(barrier, inc=1, device_id={"ctx": c, "tp": source_rank},
                                device_id_type=MESH)
    pl.semaphore_wait(barrier, 2 + pieces * ranks - own.astype(jnp.int32))

    def piece_copy(p, t):
        return pltpu.make_async_remote_copy(
            src_ref=pieces_ref.at[p], dst_ref=mine_ref.at[me],
            send_sem=piece_send.at[p * ranks + t], recv_sem=piece_recv.at[me],
            device_id={"ctx": rank * pieces + p, "tp": t}, device_id_type=MESH)

    own_piece = lax.max(me - rank * pieces, 0)
    local = pltpu.make_async_copy(
        pieces_ref.at[lax.min(own_piece, pieces - 1)], mine_ref.at[me], local_sem)

    def to_other(p, t):
        return jnp.logical_not(jnp.logical_and(rank * pieces + p == me, rank == t))

    for p in range(pieces):
        for t in range(ranks):
            @pl.when(to_other(p, t))
            def _():
                piece_copy(p, t).start()

    @pl.when(own)
    def _():
        local.start()

    mask = (lax.broadcasted_iota(jnp.int32, (width, width), 0) // head
            == lax.broadcasted_iota(jnp.int32, (width, width), 1) // head)

    def spread(rows):
        return right_terms(jnp.where(mask, jnp.concatenate([rows] * tile, axis=0), 0.0))

    for g in range(groups):
        weights[g] = spread(weights_ref[:, g * width:(g + 1) * width])

    states_view = states_ref.reshape(CHUNKS, length, units)
    cot_view = cot_ref.reshape(CHUNKS, length, units)
    full_view = full.reshape(CHUNKS, length, units)
    blank = jnp.zeros((PAD - CHUNKS, units), F32)

    def token_rows(ref, t):
        return jnp.concatenate([ref[k, pl.ds(t, 1), :] for k in range(CHUNKS)] + [blank], axis=0)

    def slopes_at(t):
        h = token_rows(states_view, t)
        return 1.0 - h * h

    s_last = slopes_at(last)
    maps[last, rows_all:, :] = s_last * token_rows(cot_view, last)
    for k in range(CHUNKS):
        maps[last, k * head:(k + 1) * head, :] = weights_ref[...] * s_last[k:k + 1, :]

    def step(i, carry):
        t = last - 1 - i
        s = slopes_at(t)
        c = token_rows(cot_view, t)
        for g in range(groups):
            lanes = slice(g * width, (g + 1) * width)
            y = dot(left_terms(maps[t + 1, :, lanes]), weights[g])
            for k in range(CHUNKS):
                rows = slice(k * head, (k + 1) * head)
                maps[t, rows, lanes] = y[rows] * s[k:k + 1, lanes]
            maps[t, rows_all:, lanes] = s[:, lanes] * (c[:, lanes] + y[rows_all:])
        return carry

    lax.fori_loop(0, last, step, 0)

    state = [None] * groups
    for k in range(CHUNKS - 1, -1, -1):
        rows = slice(k * head, (k + 1) * head)
        for g in range(groups):
            lanes = slice(g * width, (g + 1) * width)
            vec = maps[0, rows_all + k:rows_all + k + 1, lanes]
            if k == CHUNKS - 1:
                running = maps[0, rows, lanes]
            else:
                y = dot(left_terms(state[g]), spread(maps[0, rows, lanes]))
                running = y[:head]
                vec = vec + y[head:head + 1]
            state[g] = jnp.concatenate([running, jnp.broadcast_to(vec, (PAD, width))], axis=0)
            suffix[rows, lanes] = running
            suffix_vec[k:k + 1, lanes] = vec

    ones = mask.astype(F32).astype(BF16)
    ones2 = jnp.concatenate([ones, ones], axis=0)
    pick = (lax.broadcasted_iota(jnp.int32, (head, width), 1) % head
            == lax.broadcasted_iota(jnp.int32, (head, width), 0))

    def marked(row):
        high, low = halves(jnp.where(pick, jnp.broadcast_to(row, (head, width)), 0.0))
        return jnp.concatenate([high, low], axis=1)

    copy = pltpu.make_async_remote_copy(
        src_ref=e_out, dst_ref=e_in, send_sem=send_sem, recv_sem=recv_sem,
        device_id={"ctx": lax.max(me - 1, 0)}, device_id_type=MESH)

    @pl.when(me == n - 1)
    def _():
        e_in[...] = jnp.zeros_like(e_in)

    @pl.when(me < n - 1)
    def _():
        copy.wait_recv()

    spreads = []
    for g in range(groups):
        lanes = slice(g * width, (g + 1) * width)
        e = dot(marked(e_in[:, lanes]), ones2)
        spreads.append(e)
        e_out[:, lanes] = suffix_vec[0:1, lanes] + jnp.sum(
            e * suffix[0:head, lanes], axis=0, keepdims=True)

    @pl.when(me > 0)
    def _():
        copy.start()

    for g in range(groups):
        lanes = slice(g * width, (g + 1) * width)
        e = spreads[g]
        starts = [marked(suffix_vec[k:k + 1, lanes] + jnp.sum(
            e * suffix[k * head:(k + 1) * head, lanes], axis=0, keepdims=True))
            for k in range(1, CHUNKS)]
        spread_e[:rows_all - head, lanes] = dot(jnp.concatenate(starts, axis=0), ones2)
        spread_e[rows_all - head:, lanes] = e

    for k in range(CHUNKS):
        for g in range(groups):
            rows = slice(k * head, (k + 1) * head)
            lanes = slice(g * width, (g + 1) * width)
            e = spread_e[rows, lanes]

            def solve(t, carry):
                value = maps[t, rows_all + k:rows_all + k + 1, lanes] + jnp.sum(
                    maps[t, rows, lanes] * e, axis=0, keepdims=True)
                full_view[k, pl.ds(t, 1), lanes] = value
                return carry

            lax.fori_loop(0, length, solve, 0, unroll=8)
    adj_ref[...] = full[...].astype(BF16)

    @pl.when(me > 0)
    def _():
        copy.wait_send()

    for p in range(pieces):
        for t in range(ranks):
            @pl.when(to_other(p, t))
            def _():
                piece_copy(p, t).wait_send()
    for c in range(n):
        @pl.when(jnp.logical_not(jnp.logical_and(own, me == c)))
        def _():
            pltpu.make_async_remote_copy(
                src_ref=pieces_ref.at[0], dst_ref=mine_ref.at[c],
                send_sem=piece_send.at[0], recv_sem=piece_recv.at[c],
                device_id={"ctx": c, "tp": source_rank}, device_id_type=MESH).wait_recv()

    @pl.when(own)
    def _():
        local.wait()


def on_device(layer_inputs, states, cotangent, block_weights):
    tokens, units = states.shape
    heads, head, _ = block_weights.shape
    n = lax.axis_size("ctx")
    ranks = lax.axis_size("tp")
    features = layer_inputs.shape[1]
    columns = features * ranks // n
    pieces = features // columns
    length = tokens // CHUNKS
    width = min(256, units)
    flat = jnp.transpose(block_weights, (1, 0, 2)).reshape(head, units)
    cut = jnp.transpose(layer_inputs.reshape(tokens, pieces, columns), (1, 0, 2))
    vmem = pl.BlockSpec(memory_space=pltpu.VMEM)
    hbm = pl.BlockSpec(memory_space=pl.ANY)
    adj, mine = pl.pallas_call(
        recurrence,
        out_shape=(jax.ShapeDtypeStruct((tokens, units), BF16),
                   jax.ShapeDtypeStruct((n, tokens, columns), BF16)),
        in_specs=[vmem] * 3 + [hbm],
        out_specs=(vmem, hbm),
        scratch_shapes=[
            pltpu.VMEM((length, CHUNKS * head + PAD, units), F32),
            pltpu.VMEM((units // width, 3 * width, width), BF16),
            pltpu.VMEM((CHUNKS * head, units), F32),
            pltpu.VMEM((CHUNKS, units), F32),
            pltpu.VMEM((CHUNKS * head, units), F32),
            pltpu.VMEM((tokens, units), F32),
            pltpu.VMEM((1, units), F32),
            pltpu.VMEM((1, units), F32),
            pltpu.SemaphoreType.DMA,
            pltpu.SemaphoreType.DMA,
            pltpu.SemaphoreType.DMA,
            pltpu.SemaphoreType.DMA((pieces * ranks,)),
            pltpu.SemaphoreType.DMA((n,)),
        ],
        compiler_params=pltpu.CompilerParams(
            collective_id=0, has_side_effects=True, vmem_limit_bytes=48 * 1024 * 1024),
    )(states, cotangent, flat, cut)
    every = lax.all_gather(adj, "ctx", axis=0, tiled=True)
    mine = mine.reshape(n * tokens, columns)
    block = lax.dot_general(mine, every, (((0,), (0,)), ((), ())), preferred_element_type=F32)
    return lax.all_to_all(block, "tp", split_axis=0, concat_axis=1, tiled=True)


def solution(mesh):
    in_specs = (P("ctx", "tp"), P("ctx", "tp"), P("ctx", "tp"), P("tp", None, None))
    out_specs = P(("ctx", "tp"), None)
    return jax.shard_map(
        on_device, mesh=mesh, in_specs=in_specs, out_specs=out_specs, check_vma=False
    )
```

```python
import jax
import jax.numpy as jnp
from jax import lax
from jax.experimental import pallas as pl
from jax.experimental.pallas import tpu as pltpu
from jax.sharding import PartitionSpec as P

MESH = pl.DeviceIdType.MESH
CHUNKS = 8
PAD = 16
F32 = jnp.float32
BF16 = jnp.bfloat16


def halves(value):
    high = value.astype(BF16)
    low = (value - high.astype(F32)).astype(BF16)
    return high, low


def dot(left, right):
    return jnp.dot(left, right, preferred_element_type=F32)


def left_terms(value):
    high, low = halves(value)
    return jnp.concatenate([high, low, high], axis=1)


def right_terms(value):
    high, low = halves(value)
    return jnp.concatenate([high, high, low], axis=0)


def backward(states_ref, cot_ref, weights_ref, pieces_ref, out_ref,
             maps, weights, relay_weights, suffix, suffix_vec, spread_e, full, mine_ref, blocks,
             total, e_in, e_out, send_sem, recv_sem, local_sem, piece_send, piece_recv,
             line_send, pair_send, block_recv, rows_send, rows_recv):
    n = lax.axis_size("ctx")
    ranks = lax.axis_size("tp")
    me = lax.axis_index("ctx")
    rank = lax.axis_index("tp")
    tokens, units = states_ref.shape
    head = weights_ref.shape[0]
    length = tokens // CHUNKS
    width = min(256, units)
    groups = units // width
    tile = width // head
    rows_all = CHUNKS * head
    pieces = pieces_ref.shape[0]
    last = length - 1
    outer = n // 2

    barrier = pltpu.get_barrier_semaphore()
    pl.semaphore_signal(barrier, inc=1, device_id={"ctx": lax.rem(me + 1, n)}, device_id_type=MESH)
    pl.semaphore_signal(barrier, inc=1, device_id={"ctx": lax.rem(me + n - 1, n)}, device_id_type=MESH)
    source_rank = me // pieces
    own = source_rank == rank
    for c in range(n):
        @pl.when(jnp.logical_not(jnp.logical_and(own, me == c)))
        def _():
            pl.semaphore_signal(barrier, inc=1, device_id={"ctx": c, "tp": source_rank},
                                device_id_type=MESH)
    across = me + 1 - 2 * lax.rem(me, 2)
    pl.semaphore_signal(barrier, inc=1, device_id={"ctx": across}, device_id_type=MESH)
    for k in range(1, outer):
        pl.semaphore_signal(barrier, inc=1, device_id={"ctx": lax.rem(me + 2 * k, n)},
                            device_id_type=MESH)
    for k in range(1, ranks):
        pl.semaphore_signal(barrier, inc=1, device_id={"tp": lax.rem(rank + k, ranks)},
                            device_id_type=MESH)
    pl.semaphore_wait(
        barrier, 2 + 1 + outer - 1 + ranks - 1 + pieces * ranks - own.astype(jnp.int32))

    def piece_copy(p, t):
        return pltpu.make_async_remote_copy(
            src_ref=pieces_ref.at[p], dst_ref=mine_ref.at[me],
            send_sem=piece_send.at[p * ranks + t], recv_sem=piece_recv.at[me],
            device_id={"ctx": rank * pieces + p, "tp": t}, device_id_type=MESH)

    own_piece = lax.max(me - rank * pieces, 0)
    local = pltpu.make_async_copy(
        pieces_ref.at[lax.min(own_piece, pieces - 1)], mine_ref.at[me], local_sem)

    def to_other(p, t):
        return jnp.logical_not(jnp.logical_and(rank * pieces + p == me, rank == t))

    for p in range(pieces):
        for t in range(ranks):
            @pl.when(to_other(p, t))
            def _():
                piece_copy(p, t).start()

    @pl.when(own)
    def _():
        local.start()

    mask = (lax.broadcasted_iota(jnp.int32, (width, width), 0) // head
            == lax.broadcasted_iota(jnp.int32, (width, width), 1) // head)

    def spread(rows):
        return right_terms(jnp.where(mask, jnp.concatenate([rows] * tile, axis=0), 0.0))

    for g in range(groups):
        weights[g] = spread(weights_ref[:, g * width:(g + 1) * width])

    states_view = states_ref.reshape(CHUNKS, length, units)
    cot_view = cot_ref.reshape(CHUNKS, length, units)
    full_view = full.reshape(CHUNKS, length, units)
    blank = jnp.zeros((PAD - CHUNKS, units), F32)

    def token_rows(ref, t):
        return jnp.concatenate([ref[k, pl.ds(t, 1), :] for k in range(CHUNKS)] + [blank], axis=0)

    def slopes_at(t):
        h = token_rows(states_view, t)
        return 1.0 - h * h

    s_last = slopes_at(last)
    maps[last, rows_all:, :] = s_last * token_rows(cot_view, last)
    for k in range(CHUNKS):
        maps[last, k * head:(k + 1) * head, :] = weights_ref[...] * s_last[k:k + 1, :]

    def step(i, carry):
        t = last - 1 - i
        s = slopes_at(t)
        c = token_rows(cot_view, t)
        for g in range(groups):
            lanes = slice(g * width, (g + 1) * width)
            y = dot(left_terms(maps[t + 1, :, lanes]), weights[g])
            for k in range(CHUNKS):
                rows = slice(k * head, (k + 1) * head)
                maps[t, rows, lanes] = y[rows] * s[k:k + 1, lanes]
            maps[t, rows_all:, lanes] = s[:, lanes] * (c[:, lanes] + y[rows_all:])
        return carry

    lax.fori_loop(0, last, step, 0)

    state = [None] * groups
    for k in range(CHUNKS - 1, -1, -1):
        rows = slice(k * head, (k + 1) * head)
        for g in range(groups):
            lanes = slice(g * width, (g + 1) * width)
            vec = maps[0, rows_all + k:rows_all + k + 1, lanes]
            if k == CHUNKS - 1:
                running = maps[0, rows, lanes]
            else:
                y = dot(left_terms(state[g]), spread(maps[0, rows, lanes]))
                running = y[:head]
                vec = vec + y[head:head + 1]
            state[g] = jnp.concatenate([running, jnp.broadcast_to(vec, (PAD, width))], axis=0)
            suffix[rows, lanes] = running
            suffix_vec[k:k + 1, lanes] = vec

    ones = mask.astype(F32).astype(BF16)
    ones2 = jnp.concatenate([ones, ones], axis=0)
    pick = (lax.broadcasted_iota(jnp.int32, (head, width), 1) % head
            == lax.broadcasted_iota(jnp.int32, (head, width), 0))

    def marked(row):
        high, low = halves(jnp.where(pick, jnp.broadcast_to(row, (head, width)), 0.0))
        return jnp.concatenate([high, low], axis=1)

    for g in range(groups):
        relay_weights[g] = spread(suffix[0:head, g * width:(g + 1) * width])

    copy = pltpu.make_async_remote_copy(
        src_ref=e_out, dst_ref=e_in, send_sem=send_sem, recv_sem=recv_sem,
        device_id={"ctx": lax.max(me - 1, 0)}, device_id_type=MESH)

    @pl.when(me == n - 1)
    def _():
        e_in[...] = jnp.zeros_like(e_in)

    @pl.when(me < n - 1)
    def _():
        copy.wait_recv()

    for g in range(groups):
        lanes = slice(g * width, (g + 1) * width)
        e = jnp.broadcast_to(e_in[:, lanes], (PAD, width))
        e_out[:, lanes] = suffix_vec[0:1, lanes] + dot(left_terms(e), relay_weights[g])[0:1]

    @pl.when(me > 0)
    def _():
        copy.start()

    for g in range(groups):
        lanes = slice(g * width, (g + 1) * width)
        e = dot(marked(e_in[:, lanes]), ones2)
        starts = [marked(suffix_vec[k:k + 1, lanes] + jnp.sum(
            e * suffix[k * head:(k + 1) * head, lanes], axis=0, keepdims=True))
            for k in range(1, CHUNKS)]
        spread_e[:rows_all - head, lanes] = dot(jnp.concatenate(starts, axis=0), ones2)
        spread_e[rows_all - head:, lanes] = e

    def line_copy(g, o):
        return pltpu.make_async_remote_copy(
            src_ref=blocks.at[me, g], dst_ref=blocks.at[me, g],
            send_sem=line_send.at[g, o], recv_sem=block_recv.at[me, g],
            device_id={"ctx": 2 * o + lax.rem(me, 2)}, device_id_type=MESH)

    def pair_copy(g, o):
        c = 2 * o + lax.rem(me, 2)
        return pltpu.make_async_remote_copy(
            src_ref=blocks.at[c, g], dst_ref=blocks.at[c, g],
            send_sem=pair_send.at[g, o], recv_sem=block_recv.at[c, g],
            device_id={"ctx": across}, device_id_type=MESH)

    def arrived(c, g):
        pltpu.make_async_remote_copy(
            src_ref=blocks.at[c, g], dst_ref=blocks.at[c, g],
            send_sem=line_send.at[g, 0], recv_sem=block_recv.at[c, g],
            device_id={"ctx": across}, device_id_type=MESH).wait_recv()

    place = me // 2
    for g in range(groups):
        lanes = slice(g * width, (g + 1) * width)
        for k in range(CHUNKS):
            rows = slice(k * head, (k + 1) * head)
            e = spread_e[rows, lanes]

            def solve(t, carry):
                value = maps[t, rows_all + k:rows_all + k + 1, lanes] + jnp.sum(
                    maps[t, rows, lanes] * e, axis=0, keepdims=True)
                full_view[k, pl.ds(t, 1), lanes] = value
                return carry

            lax.fori_loop(0, length, solve, 0, unroll=8)
        blocks[me, g] = full[:, lanes].astype(BF16)
        pair_copy(g, place).start()

        def send(o, carry):
            @pl.when(o != place)
            def _():
                line_copy(g, o).start()
            return carry

        lax.fori_loop(0, outer, send, 0)

    @pl.when(own)
    def _():
        local.wait()

    for c in range(n):
        @pl.when(jnp.logical_not(jnp.logical_and(own, me == c)))
        def _():
            pltpu.make_async_remote_copy(
                src_ref=pieces_ref.at[0], dst_ref=mine_ref.at[c],
                send_sem=piece_send.at[0], recv_sem=piece_recv.at[c],
                device_id={"ctx": c, "tp": source_rank}, device_id_type=MESH).wait_recv()

    total[...] = jnp.zeros_like(total)

    def gather(i, carry):
        o = outer - 1 - i
        near = 2 * o + lax.rem(me, 2)
        far = 2 * o + 1 - lax.rem(me, 2)

        @pl.when(o != place)
        def _():
            for g in range(groups):
                arrived(near, g)
                pair_copy(g, o).start()

        for c in (near, far):
            for g in range(groups):
                lanes = slice(g * width, (g + 1) * width)
                if c is far:
                    arrived(far, g)
                total[:, lanes] += dot(mine_ref[c], blocks[c, g])
        return carry

    lax.fori_loop(0, outer, gather, 0)

    share = total.shape[0] // ranks

    def rows_copy(t, source):
        return pltpu.make_async_remote_copy(
            src_ref=total.at[pl.ds(t * share, share)],
            dst_ref=out_ref.at[:, pl.ds(pl.multiple_of(source * units, 128), units)],
            send_sem=rows_send.at[t], recv_sem=rows_recv.at[source],
            device_id={"tp": t}, device_id_type=MESH)

    for k in range(1, ranks):
        rows_copy(lax.rem(rank + k, ranks), rank).start()
    out_ref[:, pl.ds(pl.multiple_of(rank * units, 128), units)] = total[
        pl.ds(pl.multiple_of(rank * share, 8), share), :]

    @pl.when(me > 0)
    def _():
        copy.wait_send()

    for p in range(pieces):
        for t in range(ranks):
            @pl.when(to_other(p, t))
            def _():
                piece_copy(p, t).wait_send()

    def drain(o, carry):
        for g in range(groups):
            pair_copy(g, o).wait_send()

            @pl.when(o != place)
            def _():
                line_copy(g, o).wait_send()
        return carry

    lax.fori_loop(0, outer, drain, 0)
    for k in range(1, ranks):
        t = lax.rem(rank + k, ranks)
        rows_copy(t, t).wait_recv()
        rows_copy(t, rank).wait_send()


def on_device(layer_inputs, states, cotangent, block_weights):
    tokens, units = states.shape
    heads, head, _ = block_weights.shape
    n = lax.axis_size("ctx")
    ranks = lax.axis_size("tp")
    features = layer_inputs.shape[1]
    columns = features * ranks // n
    pieces = features // columns
    length = tokens // CHUNKS
    width = min(256, units)
    flat = jnp.transpose(block_weights, (1, 0, 2)).reshape(head, units)
    cut = jnp.transpose(layer_inputs).reshape(pieces, columns, tokens)
    groups = units // width
    vmem = pl.BlockSpec(memory_space=pltpu.VMEM)
    return pl.pallas_call(
        backward,
        out_shape=jax.ShapeDtypeStruct((columns // ranks, units * ranks), F32),
        in_specs=[vmem] * 4,
        out_specs=vmem,
        scratch_shapes=[
            pltpu.VMEM((length, CHUNKS * head + PAD, units), F32),
            pltpu.VMEM((groups, 3 * width, width), BF16),
            pltpu.VMEM((groups, 3 * width, width), BF16),
            pltpu.VMEM((CHUNKS * head, units), F32),
            pltpu.VMEM((CHUNKS, units), F32),
            pltpu.VMEM((CHUNKS * head, units), F32),
            pltpu.VMEM((tokens, units), F32),
            pltpu.VMEM((n, columns, tokens), BF16),
            pltpu.VMEM((n, groups, tokens, width), BF16),
            pltpu.VMEM((columns, units), F32),
            pltpu.VMEM((1, units), F32),
            pltpu.VMEM((1, units), F32),
            pltpu.SemaphoreType.DMA,
            pltpu.SemaphoreType.DMA,
            pltpu.SemaphoreType.DMA,
            pltpu.SemaphoreType.DMA((pieces * ranks,)),
            pltpu.SemaphoreType.DMA((n,)),
            pltpu.SemaphoreType.DMA((groups, n // 2)),
            pltpu.SemaphoreType.DMA((groups, n // 2)),
            pltpu.SemaphoreType.DMA((n, groups)),
            pltpu.SemaphoreType.DMA((ranks,)),
            pltpu.SemaphoreType.DMA((ranks,)),
        ],
        compiler_params=pltpu.CompilerParams(
            collective_id=0, has_side_effects=True, vmem_limit_bytes=48 * 1024 * 1024),
    )(states, cotangent, flat, cut)


def solution(mesh):
    in_specs = (P("ctx", "tp"), P("ctx", "tp"), P("ctx", "tp"), P("tp", None, None))
    out_specs = P(("ctx", "tp"), None)
    return jax.shard_map(
        on_device, mesh=mesh, in_specs=in_specs, out_specs=out_specs, check_vma=False
    )
```

```python
import jax
import jax.numpy as jnp
from jax import lax
from jax.experimental import pallas as pl
from jax.experimental.pallas import tpu as pltpu
from jax.sharding import PartitionSpec as P

MESH = pl.DeviceIdType.MESH
CHUNKS = 8
PAD = 16
F32 = jnp.float32
BF16 = jnp.bfloat16


def halves(value):
    high = value.astype(BF16)
    low = (value - high.astype(F32)).astype(BF16)
    return high, low


def dot(left, right):
    return jnp.dot(left, right, preferred_element_type=F32)


def left_terms(value):
    high, low = halves(value)
    return jnp.concatenate([high, low, high], axis=1)


def right_terms(value):
    high, low = halves(value)
    return jnp.concatenate([high, high, low], axis=0)


def backward(states_ref, cot_ref, weights_ref, pieces_ref, out_ref,
             maps, weights, relay_weights, suffix, suffix_vec, spread_e, full, mine_ref, blocks,
             total, e_in, e_out, send_sem, recv_sem, local_sem, piece_send, piece_recv,
             mine_send, mine_recv, line_send, pair_send, block_recv, rows_send, rows_recv):
    n = lax.axis_size("ctx")
    ranks = lax.axis_size("tp")
    me = lax.axis_index("ctx")
    rank = lax.axis_index("tp")
    tokens, units = states_ref.shape
    head = weights_ref.shape[0]
    length = tokens // CHUNKS
    width = min(256, units)
    groups = units // width
    tile = width // head
    rows_all = CHUNKS * head
    pieces = pieces_ref.shape[0]
    last = length - 1
    outer = n // 2

    barrier = pltpu.get_barrier_semaphore()
    pl.semaphore_signal(barrier, inc=1, device_id={"ctx": lax.rem(me + 1, n)}, device_id_type=MESH)
    pl.semaphore_signal(barrier, inc=1, device_id={"ctx": lax.rem(me + n - 1, n)}, device_id_type=MESH)
    own = me // pieces == rank

    @pl.when(own)
    def _():
        for k in range(1, n):
            pl.semaphore_signal(barrier, inc=1, device_id={"ctx": lax.rem(me + k, n)},
                                device_id_type=MESH)
    across = me + 1 - 2 * lax.rem(me, 2)
    pl.semaphore_signal(barrier, inc=1, device_id={"ctx": across}, device_id_type=MESH)
    for k in range(1, outer):
        pl.semaphore_signal(barrier, inc=1, device_id={"ctx": lax.rem(me + 2 * k, n)},
                            device_id_type=MESH)
    for k in range(1, ranks):
        pl.semaphore_signal(barrier, inc=1, device_id={"tp": lax.rem(rank + k, ranks)},
                            device_id_type=MESH)
    pl.semaphore_wait(
        barrier, 2 + 1 + outer - 1 + ranks - 1 + pieces - own.astype(jnp.int32))

    def piece_copy(p):
        return pltpu.make_async_remote_copy(
            src_ref=pieces_ref.at[p], dst_ref=mine_ref.at[me],
            send_sem=piece_send.at[p], recv_sem=piece_recv.at[me],
            device_id={"ctx": rank * pieces + p}, device_id_type=MESH)

    own_piece = lax.max(me - rank * pieces, 0)
    local = pltpu.make_async_copy(
        pieces_ref.at[lax.min(own_piece, pieces - 1)], mine_ref.at[me], local_sem)

    for p in range(pieces):
        @pl.when(rank * pieces + p != me)
        def _():
            piece_copy(p).start()

    @pl.when(own)
    def _():
        local.start()

    def mine_copy(k):
        return pltpu.make_async_remote_copy(
            src_ref=mine_ref, dst_ref=mine_ref,
            send_sem=mine_send.at[k], recv_sem=mine_recv,
            device_id={"tp": lax.rem(rank + k, ranks)}, device_id_type=MESH)

    mask = (lax.broadcasted_iota(jnp.int32, (width, width), 0) // head
            == lax.broadcasted_iota(jnp.int32, (width, width), 1) // head)

    def spread(rows):
        return right_terms(jnp.where(mask, jnp.concatenate([rows] * tile, axis=0), 0.0))

    for g in range(groups):
        weights[g] = spread(weights_ref[:, g * width:(g + 1) * width])

    states_view = states_ref.reshape(CHUNKS, length, units)
    cot_view = cot_ref.reshape(CHUNKS, length, units)
    full_view = full.reshape(CHUNKS, length, units)
    blank = jnp.zeros((PAD - CHUNKS, units), F32)

    def token_rows(ref, t):
        return jnp.concatenate([ref[k, pl.ds(t, 1), :] for k in range(CHUNKS)] + [blank], axis=0)

    def slopes_at(t):
        h = token_rows(states_view, t)
        return 1.0 - h * h

    s_last = slopes_at(last)
    maps[last, rows_all:, :] = s_last * token_rows(cot_view, last)
    for k in range(CHUNKS):
        maps[last, k * head:(k + 1) * head, :] = weights_ref[...] * s_last[k:k + 1, :]

    def step(i, carry):
        t = last - 1 - i
        s = slopes_at(t)
        c = token_rows(cot_view, t)
        for g in range(groups):
            lanes = slice(g * width, (g + 1) * width)
            y = dot(left_terms(maps[t + 1, :, lanes]), weights[g])
            for k in range(CHUNKS):
                rows = slice(k * head, (k + 1) * head)
                maps[t, rows, lanes] = y[rows] * s[k:k + 1, lanes]
            maps[t, rows_all:, lanes] = s[:, lanes] * (c[:, lanes] + y[rows_all:])
        return carry

    lax.fori_loop(0, last, step, 0)

    @pl.when(own)
    def _():
        local.wait()
        for k in range(1, n):
            c = lax.rem(me + k, n)
            pltpu.make_async_remote_copy(
                src_ref=pieces_ref.at[0], dst_ref=mine_ref.at[c],
                send_sem=piece_send.at[0], recv_sem=piece_recv.at[c],
                device_id={"ctx": c}, device_id_type=MESH).wait_recv()
        for k in range(1, ranks):
            mine_copy(k).start()

    state = [None] * groups
    for k in range(CHUNKS - 1, -1, -1):
        rows = slice(k * head, (k + 1) * head)
        for g in range(groups):
            lanes = slice(g * width, (g + 1) * width)
            vec = maps[0, rows_all + k:rows_all + k + 1, lanes]
            if k == CHUNKS - 1:
                running = maps[0, rows, lanes]
            else:
                y = dot(left_terms(state[g]), spread(maps[0, rows, lanes]))
                running = y[:head]
                vec = vec + y[head:head + 1]
            state[g] = jnp.concatenate([running, jnp.broadcast_to(vec, (PAD, width))], axis=0)
            suffix[rows, lanes] = running
            suffix_vec[k:k + 1, lanes] = vec

    ones = mask.astype(F32).astype(BF16)
    ones2 = jnp.concatenate([ones, ones], axis=0)
    pick = (lax.broadcasted_iota(jnp.int32, (head, width), 1) % head
            == lax.broadcasted_iota(jnp.int32, (head, width), 0))

    def marked(row):
        high, low = halves(jnp.where(pick, jnp.broadcast_to(row, (head, width)), 0.0))
        return jnp.concatenate([high, low], axis=1)

    for g in range(groups):
        relay_weights[g] = spread(suffix[0:head, g * width:(g + 1) * width])

    copy = pltpu.make_async_remote_copy(
        src_ref=e_out, dst_ref=e_in, send_sem=send_sem, recv_sem=recv_sem,
        device_id={"ctx": lax.max(me - 1, 0)}, device_id_type=MESH)

    @pl.when(me == n - 1)
    def _():
        e_in[...] = jnp.zeros_like(e_in)

    @pl.when(me < n - 1)
    def _():
        copy.wait_recv()

    for g in range(groups):
        lanes = slice(g * width, (g + 1) * width)
        e = jnp.broadcast_to(e_in[:, lanes], (PAD, width))
        e_out[:, lanes] = suffix_vec[0:1, lanes] + dot(left_terms(e), relay_weights[g])[0:1]

    @pl.when(me > 0)
    def _():
        copy.start()

    for g in range(groups):
        lanes = slice(g * width, (g + 1) * width)
        e = dot(marked(e_in[:, lanes]), ones2)
        starts = [marked(suffix_vec[k:k + 1, lanes] + jnp.sum(
            e * suffix[k * head:(k + 1) * head, lanes], axis=0, keepdims=True))
            for k in range(1, CHUNKS)]
        spread_e[:rows_all - head, lanes] = dot(jnp.concatenate(starts, axis=0), ones2)
        spread_e[rows_all - head:, lanes] = e

    def line_copy(g, o):
        return pltpu.make_async_remote_copy(
            src_ref=blocks.at[me, g], dst_ref=blocks.at[me, g],
            send_sem=line_send.at[g, o], recv_sem=block_recv.at[me, g],
            device_id={"ctx": 2 * o + lax.rem(me, 2)}, device_id_type=MESH)

    def pair_copy(g, o):
        c = 2 * o + lax.rem(me, 2)
        return pltpu.make_async_remote_copy(
            src_ref=blocks.at[c, g], dst_ref=blocks.at[c, g],
            send_sem=pair_send.at[g, o], recv_sem=block_recv.at[c, g],
            device_id={"ctx": across}, device_id_type=MESH)

    def arrived(c, g):
        pltpu.make_async_remote_copy(
            src_ref=blocks.at[c, g], dst_ref=blocks.at[c, g],
            send_sem=line_send.at[g, 0], recv_sem=block_recv.at[c, g],
            device_id={"ctx": across}, device_id_type=MESH).wait_recv()

    place = me // 2
    for g in range(groups):
        lanes = slice(g * width, (g + 1) * width)
        for k in range(CHUNKS):
            rows = slice(k * head, (k + 1) * head)
            e = spread_e[rows, lanes]

            def solve(t, carry):
                value = maps[t, rows_all + k:rows_all + k + 1, lanes] + jnp.sum(
                    maps[t, rows, lanes] * e, axis=0, keepdims=True)
                full_view[k, pl.ds(t, 1), lanes] = value
                return carry

            lax.fori_loop(0, length, solve, 0, unroll=8)
        blocks[me, g] = full[:, lanes].astype(BF16)
        pair_copy(g, place).start()

        def send(o, carry):
            @pl.when(o != place)
            def _():
                line_copy(g, o).start()
            return carry

        lax.fori_loop(0, outer, send, 0)

    @pl.when(jnp.logical_not(own))
    def _():
        mine_copy(1).wait_recv()

    total[...] = jnp.zeros_like(total)

    def gather(i, carry):
        o = outer - 1 - i
        near = 2 * o + lax.rem(me, 2)
        far = 2 * o + 1 - lax.rem(me, 2)

        @pl.when(o != place)
        def _():
            for g in range(groups):
                arrived(near, g)
                pair_copy(g, o).start()

        for c in (near, far):
            for g in range(groups):
                lanes = slice(g * width, (g + 1) * width)
                if c is far:
                    arrived(far, g)
                total[:, lanes] += dot(mine_ref[c], blocks[c, g])
        return carry

    lax.fori_loop(0, outer, gather, 0)

    share = total.shape[0] // ranks

    def rows_copy(t, source):
        return pltpu.make_async_remote_copy(
            src_ref=total.at[pl.ds(t * share, share)],
            dst_ref=out_ref.at[:, pl.ds(pl.multiple_of(source * units, 128), units)],
            send_sem=rows_send.at[t], recv_sem=rows_recv.at[source],
            device_id={"tp": t}, device_id_type=MESH)

    for k in range(1, ranks):
        rows_copy(lax.rem(rank + k, ranks), rank).start()
    out_ref[:, pl.ds(pl.multiple_of(rank * units, 128), units)] = total[
        pl.ds(pl.multiple_of(rank * share, 8), share), :]

    @pl.when(me > 0)
    def _():
        copy.wait_send()

    for p in range(pieces):
        @pl.when(rank * pieces + p != me)
        def _():
            piece_copy(p).wait_send()

    @pl.when(own)
    def _():
        for k in range(1, ranks):
            mine_copy(k).wait_send()

    def drain(o, carry):
        for g in range(groups):
            pair_copy(g, o).wait_send()

            @pl.when(o != place)
            def _():
                line_copy(g, o).wait_send()
        return carry

    lax.fori_loop(0, outer, drain, 0)
    for k in range(1, ranks):
        t = lax.rem(rank + k, ranks)
        rows_copy(t, t).wait_recv()
        rows_copy(t, rank).wait_send()


def on_device(layer_inputs, states, cotangent, block_weights):
    tokens, units = states.shape
    heads, head, _ = block_weights.shape
    n = lax.axis_size("ctx")
    ranks = lax.axis_size("tp")
    features = layer_inputs.shape[1]
    columns = features * ranks // n
    pieces = features // columns
    length = tokens // CHUNKS
    width = min(256, units)
    flat = jnp.transpose(block_weights, (1, 0, 2)).reshape(head, units)
    cut = jnp.transpose(layer_inputs).reshape(pieces, columns, tokens)
    groups = units // width
    vmem = pl.BlockSpec(memory_space=pltpu.VMEM)
    return pl.pallas_call(
        backward,
        out_shape=jax.ShapeDtypeStruct((columns // ranks, units * ranks), F32),
        in_specs=[vmem] * 4,
        out_specs=vmem,
        scratch_shapes=[
            pltpu.VMEM((length, CHUNKS * head + PAD, units), F32),
            pltpu.VMEM((groups, 3 * width, width), BF16),
            pltpu.VMEM((groups, 3 * width, width), BF16),
            pltpu.VMEM((CHUNKS * head, units), F32),
            pltpu.VMEM((CHUNKS, units), F32),
            pltpu.VMEM((CHUNKS * head, units), F32),
            pltpu.VMEM((tokens, units), F32),
            pltpu.VMEM((n, columns, tokens), BF16),
            pltpu.VMEM((n, groups, tokens, width), BF16),
            pltpu.VMEM((columns, units), F32),
            pltpu.VMEM((1, units), F32),
            pltpu.VMEM((1, units), F32),
            pltpu.SemaphoreType.DMA,
            pltpu.SemaphoreType.DMA,
            pltpu.SemaphoreType.DMA,
            pltpu.SemaphoreType.DMA((pieces,)),
            pltpu.SemaphoreType.DMA((n,)),
            pltpu.SemaphoreType.DMA((ranks,)),
            pltpu.SemaphoreType.DMA,
            pltpu.SemaphoreType.DMA((groups, n // 2)),
            pltpu.SemaphoreType.DMA((groups, n // 2)),
            pltpu.SemaphoreType.DMA((n, groups)),
            pltpu.SemaphoreType.DMA((ranks,)),
            pltpu.SemaphoreType.DMA((ranks,)),
        ],
        compiler_params=pltpu.CompilerParams(
            collective_id=0, has_side_effects=True, vmem_limit_bytes=48 * 1024 * 1024),
    )(states, cotangent, flat, cut)


def solution(mesh):
    in_specs = (P("ctx", "tp"), P("ctx", "tp"), P("ctx", "tp"), P("tp", None, None))
    out_specs = P(("ctx", "tp"), None)
    return jax.shard_map(
        on_device, mesh=mesh, in_specs=in_specs, out_specs=out_specs, check_vma=False
    )
```

```python
import jax
import jax.numpy as jnp
from jax import lax
from jax.experimental import pallas as pl
from jax.experimental.pallas import tpu as pltpu
from jax.sharding import PartitionSpec as P

MESH = pl.DeviceIdType.MESH
CHUNKS = 8
PAD = 16
F32 = jnp.float32
BF16 = jnp.bfloat16


def halves(value):
    high = value.astype(BF16)
    low = (value - high.astype(F32)).astype(BF16)
    return high, low


def dot(left, right):
    return jnp.dot(left, right, preferred_element_type=F32)


def left_terms(value):
    high, low = halves(value)
    return jnp.concatenate([high, low, high], axis=1)


def right_terms(value):
    high, low = halves(value)
    return jnp.concatenate([high, high, low], axis=0)


def backward(states_ref, cot_ref, weights_ref, pieces_ref, out_ref,
             maps, weights, relay_weights, suffix, suffix_vec, spread_e, full, mine_ref, blocks,
             total, e_in, e_out, send_sem, recv_sem, local_sem, piece_send, piece_recv,
             mine_send, mine_recv, line_send, pair_send, block_recv, rows_send, rows_recv):
    n = lax.axis_size("ctx")
    ranks = lax.axis_size("tp")
    me = lax.axis_index("ctx")
    rank = lax.axis_index("tp")
    tokens, units = states_ref.shape
    head = weights_ref.shape[0]
    length = tokens // CHUNKS
    width = min(256, units)
    groups = units // width
    tile = width // head
    rows_all = CHUNKS * head
    pieces = pieces_ref.shape[0]
    last = length - 1
    outer = n // 2

    barrier = pltpu.get_barrier_semaphore()
    pl.semaphore_signal(barrier, inc=1, device_id={"ctx": lax.rem(me + 1, n)}, device_id_type=MESH)
    pl.semaphore_signal(barrier, inc=1, device_id={"ctx": lax.rem(me + n - 1, n)}, device_id_type=MESH)
    own = me // pieces == rank

    @pl.when(own)
    def _():
        for k in range(1, n):
            pl.semaphore_signal(barrier, inc=1, device_id={"ctx": lax.rem(me + k, n)},
                                device_id_type=MESH)
    across = me + 1 - 2 * lax.rem(me, 2)
    pl.semaphore_signal(barrier, inc=1, device_id={"ctx": across}, device_id_type=MESH)
    for k in range(1, outer):
        pl.semaphore_signal(barrier, inc=1, device_id={"ctx": lax.rem(me + 2 * k, n)},
                            device_id_type=MESH)
    for k in range(1, ranks):
        pl.semaphore_signal(barrier, inc=1, device_id={"tp": lax.rem(rank + k, ranks)},
                            device_id_type=MESH)
    pl.semaphore_wait(
        barrier, 2 + 1 + outer - 1 + ranks - 1 + pieces - own.astype(jnp.int32))

    def piece_copy(p):
        return pltpu.make_async_remote_copy(
            src_ref=pieces_ref.at[p], dst_ref=mine_ref.at[me],
            send_sem=piece_send.at[p], recv_sem=piece_recv.at[me],
            device_id={"ctx": rank * pieces + p}, device_id_type=MESH)

    own_piece = lax.max(me - rank * pieces, 0)
    local = pltpu.make_async_copy(
        pieces_ref.at[lax.min(own_piece, pieces - 1)], mine_ref.at[me], local_sem)

    for p in range(pieces):
        @pl.when(rank * pieces + p != me)
        def _():
            piece_copy(p).start()

    @pl.when(own)
    def _():
        local.start()

    def mine_copy(k):
        return pltpu.make_async_remote_copy(
            src_ref=mine_ref, dst_ref=mine_ref,
            send_sem=mine_send.at[k], recv_sem=mine_recv,
            device_id={"tp": lax.rem(rank + k, ranks)}, device_id_type=MESH)

    mask = (lax.broadcasted_iota(jnp.int32, (width, width), 0) // head
            == lax.broadcasted_iota(jnp.int32, (width, width), 1) // head)

    def spread(rows):
        return right_terms(jnp.where(mask, jnp.concatenate([rows] * tile, axis=0), 0.0))

    for g in range(groups):
        weights[g] = spread(weights_ref[:, g * width:(g + 1) * width])

    states_view = states_ref.reshape(CHUNKS, length, units)
    cot_view = cot_ref.reshape(CHUNKS, length, units)
    full_view = full.reshape(CHUNKS, length, units)
    blank = jnp.zeros((PAD - CHUNKS, units), F32)

    def token_rows(ref, t):
        return jnp.concatenate([ref[k, pl.ds(t, 1), :] for k in range(CHUNKS)] + [blank], axis=0)

    def slopes_at(t):
        h = token_rows(states_view, t)
        return 1.0 - h * h

    s_last = slopes_at(last)
    maps[last, rows_all:, :] = s_last * token_rows(cot_view, last)
    for k in range(CHUNKS):
        maps[last, k * head:(k + 1) * head, :] = weights_ref[...] * s_last[k:k + 1, :]

    def step(i, carry):
        t = last - 1 - i
        s = slopes_at(t)
        c = token_rows(cot_view, t)
        for g in range(groups):
            lanes = slice(g * width, (g + 1) * width)
            y = dot(left_terms(maps[t + 1, :, lanes]), weights[g])
            for k in range(CHUNKS):
                rows = slice(k * head, (k + 1) * head)
                maps[t, rows, lanes] = y[rows] * s[k:k + 1, lanes]
            maps[t, rows_all:, lanes] = s[:, lanes] * (c[:, lanes] + y[rows_all:])
        return carry

    lax.fori_loop(0, last, step, 0)

    @pl.when(own)
    def _():
        local.wait()
        for k in range(1, n):
            c = lax.rem(me + k, n)
            pltpu.make_async_remote_copy(
                src_ref=pieces_ref.at[0], dst_ref=mine_ref.at[c],
                send_sem=piece_send.at[0], recv_sem=piece_recv.at[c],
                device_id={"ctx": c}, device_id_type=MESH).wait_recv()
        for k in range(1, ranks):
            mine_copy(k).start()

    state = [None] * groups
    for k in range(CHUNKS - 1, -1, -1):
        rows = slice(k * head, (k + 1) * head)
        for g in range(groups):
            lanes = slice(g * width, (g + 1) * width)
            vec = maps[0, rows_all + k:rows_all + k + 1, lanes]
            if k == CHUNKS - 1:
                running = maps[0, rows, lanes]
            else:
                y = dot(left_terms(state[g]), spread(maps[0, rows, lanes]))
                running = y[:head]
                vec = vec + y[head:head + 1]
            state[g] = jnp.concatenate([running, jnp.broadcast_to(vec, (PAD, width))], axis=0)
            suffix[rows, lanes] = running
            suffix_vec[k:k + 1, lanes] = vec

    ones = mask.astype(F32).astype(BF16)
    ones2 = jnp.concatenate([ones, ones], axis=0)
    pick = (lax.broadcasted_iota(jnp.int32, (head, width), 1) % head
            == lax.broadcasted_iota(jnp.int32, (head, width), 0))

    def marked(row):
        high, low = halves(jnp.where(pick, jnp.broadcast_to(row, (head, width)), 0.0))
        return jnp.concatenate([high, low], axis=1)

    for g in range(groups):
        relay_weights[g] = spread(suffix[0:head, g * width:(g + 1) * width])

    copy = pltpu.make_async_remote_copy(
        src_ref=e_out, dst_ref=e_in, send_sem=send_sem, recv_sem=recv_sem,
        device_id={"ctx": lax.max(me - 1, 0)}, device_id_type=MESH)

    @pl.when(me == n - 1)
    def _():
        e_in[...] = jnp.zeros_like(e_in)

    @pl.when(me < n - 1)
    def _():
        copy.wait_recv()

    for g in range(groups):
        lanes = slice(g * width, (g + 1) * width)
        e = jnp.broadcast_to(e_in[:, lanes], (PAD, width))
        e_out[:, lanes] = suffix_vec[0:1, lanes] + dot(left_terms(e), relay_weights[g])[0:1]

    @pl.when(me > 0)
    def _():
        copy.start()

    for g in range(groups):
        lanes = slice(g * width, (g + 1) * width)
        e = dot(marked(e_in[:, lanes]), ones2)
        starts = [marked(suffix_vec[k:k + 1, lanes] + jnp.sum(
            e * suffix[k * head:(k + 1) * head, lanes], axis=0, keepdims=True))
            for k in range(1, CHUNKS)]
        spread_e[:rows_all - head, lanes] = dot(jnp.concatenate(starts, axis=0), ones2)
        spread_e[rows_all - head:, lanes] = e

    def line_copy(g, o):
        return pltpu.make_async_remote_copy(
            src_ref=blocks.at[me, g], dst_ref=blocks.at[me, g],
            send_sem=line_send.at[g, o], recv_sem=block_recv.at[me, g],
            device_id={"ctx": 2 * o + lax.rem(me, 2)}, device_id_type=MESH)

    def pair_copy(g, o):
        c = 2 * o + lax.rem(me, 2)
        return pltpu.make_async_remote_copy(
            src_ref=blocks.at[c, g], dst_ref=blocks.at[c, g],
            send_sem=pair_send.at[g, o], recv_sem=block_recv.at[c, g],
            device_id={"ctx": across}, device_id_type=MESH)

    def arrived(c, g):
        pltpu.make_async_remote_copy(
            src_ref=blocks.at[c, g], dst_ref=blocks.at[c, g],
            send_sem=line_send.at[g, 0], recv_sem=block_recv.at[c, g],
            device_id={"ctx": across}, device_id_type=MESH).wait_recv()

    place = me // 2
    for g in range(groups):
        lanes = slice(g * width, (g + 1) * width)
        for k in range(CHUNKS):
            rows = slice(k * head, (k + 1) * head)
            e = spread_e[rows, lanes]

            def solve(t, carry):
                value = maps[t, rows_all + k:rows_all + k + 1, lanes] + jnp.sum(
                    maps[t, rows, lanes] * e, axis=0, keepdims=True)
                full_view[k, pl.ds(t, 1), lanes] = value
                return carry

            lax.fori_loop(0, length, solve, 0, unroll=8)
        blocks[me, g] = full[:, lanes].astype(BF16)
        pair_copy(g, place).start()

        def send(o, carry):
            @pl.when(o != place)
            def _():
                line_copy(g, o).start()
            return carry

        lax.fori_loop(0, outer, send, 0)

    @pl.when(jnp.logical_not(own))
    def _():
        mine_copy(1).wait_recv()

    total[...] = jnp.zeros_like(total)

    def gather(i, carry):
        o = outer - 1 - i
        near = 2 * o + lax.rem(me, 2)

        @pl.when(o != place)
        def _():
            for g in range(groups):
                arrived(near, g)
                pair_copy(g, o).start()

        for g in range(groups):
            total[:, g * width:(g + 1) * width] += dot(mine_ref[near], blocks[near, g])
        return carry

    lax.fori_loop(0, outer, gather, 0)

    share = total.shape[0] // ranks

    def rows_copy(t, source, g):
        start = pl.multiple_of(source * units + g * width, 128)
        return pltpu.make_async_remote_copy(
            src_ref=total.at[pl.ds(t * share, share), pl.ds(g * width, width)],
            dst_ref=out_ref.at[:, pl.ds(start, width)],
            send_sem=rows_send.at[g, t], recv_sem=rows_recv.at[g, source],
            device_id={"tp": t}, device_id_type=MESH)

    for g in range(groups):
        lanes = slice(g * width, (g + 1) * width)

        def collect(i, carry):
            far = 2 * (outer - 1 - i) + 1 - lax.rem(me, 2)
            arrived(far, g)
            total[:, lanes] += dot(mine_ref[far], blocks[far, g])
            return carry

        lax.fori_loop(0, outer, collect, 0)
        for k in range(1, ranks):
            rows_copy(lax.rem(rank + k, ranks), rank, g).start()
        out_ref[:, pl.ds(pl.multiple_of(rank * units + g * width, 128), width)] = total[
            pl.ds(pl.multiple_of(rank * share, 8), share), lanes]

    @pl.when(me > 0)
    def _():
        copy.wait_send()

    for p in range(pieces):
        @pl.when(rank * pieces + p != me)
        def _():
            piece_copy(p).wait_send()

    @pl.when(own)
    def _():
        for k in range(1, ranks):
            mine_copy(k).wait_send()

    def drain(o, carry):
        for g in range(groups):
            pair_copy(g, o).wait_send()

            @pl.when(o != place)
            def _():
                line_copy(g, o).wait_send()
        return carry

    lax.fori_loop(0, outer, drain, 0)
    for k in range(1, ranks):
        t = lax.rem(rank + k, ranks)
        for g in range(groups):
            rows_copy(t, t, g).wait_recv()
            rows_copy(t, rank, g).wait_send()


def on_device(layer_inputs, states, cotangent, block_weights):
    tokens, units = states.shape
    heads, head, _ = block_weights.shape
    n = lax.axis_size("ctx")
    ranks = lax.axis_size("tp")
    features = layer_inputs.shape[1]
    columns = features * ranks // n
    pieces = features // columns
    length = tokens // CHUNKS
    width = min(256, units)
    flat = jnp.transpose(block_weights, (1, 0, 2)).reshape(head, units)
    cut = jnp.transpose(layer_inputs).reshape(pieces, columns, tokens)
    groups = units // width
    vmem = pl.BlockSpec(memory_space=pltpu.VMEM)
    return pl.pallas_call(
        backward,
        out_shape=jax.ShapeDtypeStruct((columns // ranks, units * ranks), F32),
        in_specs=[vmem] * 4,
        out_specs=vmem,
        scratch_shapes=[
            pltpu.VMEM((length, CHUNKS * head + PAD, units), F32),
            pltpu.VMEM((groups, 3 * width, width), BF16),
            pltpu.VMEM((groups, 3 * width, width), BF16),
            pltpu.VMEM((CHUNKS * head, units), F32),
            pltpu.VMEM((CHUNKS, units), F32),
            pltpu.VMEM((CHUNKS * head, units), F32),
            pltpu.VMEM((tokens, units), F32),
            pltpu.VMEM((n, columns, tokens), BF16),
            pltpu.VMEM((n, groups, tokens, width), BF16),
            pltpu.VMEM((columns, units), F32),
            pltpu.VMEM((1, units), F32),
            pltpu.VMEM((1, units), F32),
            pltpu.SemaphoreType.DMA,
            pltpu.SemaphoreType.DMA,
            pltpu.SemaphoreType.DMA,
            pltpu.SemaphoreType.DMA((pieces,)),
            pltpu.SemaphoreType.DMA((n,)),
            pltpu.SemaphoreType.DMA((ranks,)),
            pltpu.SemaphoreType.DMA,
            pltpu.SemaphoreType.DMA((groups, n // 2)),
            pltpu.SemaphoreType.DMA((groups, n // 2)),
            pltpu.SemaphoreType.DMA((n, groups)),
            pltpu.SemaphoreType.DMA((groups, ranks)),
            pltpu.SemaphoreType.DMA((groups, ranks)),
        ],
        compiler_params=pltpu.CompilerParams(
            collective_id=0, has_side_effects=True, vmem_limit_bytes=48 * 1024 * 1024),
    )(states, cotangent, flat, cut)


def solution(mesh):
    in_specs = (P("ctx", "tp"), P("ctx", "tp"), P("ctx", "tp"), P("tp", None, None))
    out_specs = P(("ctx", "tp"), None)
    return jax.shard_map(
        on_device, mesh=mesh, in_specs=in_specs, out_specs=out_specs, check_vma=False
    )
```

```python
import jax
import jax.numpy as jnp
from jax import lax
from jax.experimental import pallas as pl
from jax.experimental.pallas import tpu as pltpu
from jax.sharding import PartitionSpec as P

MESH = pl.DeviceIdType.MESH
CHUNKS = 8
PAD = 16
F32 = jnp.float32
BF16 = jnp.bfloat16


def halves(value):
    high = value.astype(BF16)
    low = (value - high.astype(F32)).astype(BF16)
    return high, low


def dot(left, right):
    return jnp.dot(left, right, preferred_element_type=F32)


def left_terms(value):
    high, low = halves(value)
    return jnp.concatenate([high, low, high], axis=1)


def right_terms(value):
    high, low = halves(value)
    return jnp.concatenate([high, high, low], axis=0)


def backward(states_ref, cot_ref, weights_ref, pieces_ref, out_ref,
             maps, weights, relay_weights, suffix, suffix_vec, spread_e, full, mine_ref, blocks,
             total, e_in, e_out, send_sem, recv_sem, local_sem, piece_send, piece_recv,
             mine_send, mine_recv, line_send, far_send, pair_send, block_recv, rows_send, rows_recv):
    n = lax.axis_size("ctx")
    ranks = lax.axis_size("tp")
    me = lax.axis_index("ctx")
    rank = lax.axis_index("tp")
    tokens, units = states_ref.shape
    head = weights_ref.shape[0]
    length = tokens // CHUNKS
    width = min(256, units)
    groups = units // width
    tile = width // head
    rows_all = CHUNKS * head
    pieces = pieces_ref.shape[0]
    last = length - 1
    outer = n // 2

    barrier = pltpu.get_barrier_semaphore()
    pl.semaphore_signal(barrier, inc=1, device_id={"ctx": lax.rem(me + 1, n)}, device_id_type=MESH)
    pl.semaphore_signal(barrier, inc=1, device_id={"ctx": lax.rem(me + n - 1, n)}, device_id_type=MESH)
    own = me // pieces == rank

    @pl.when(own)
    def _():
        for k in range(1, n):
            pl.semaphore_signal(barrier, inc=1, device_id={"ctx": lax.rem(me + k, n)},
                                device_id_type=MESH)
    across = me + 1 - 2 * lax.rem(me, 2)
    pl.semaphore_signal(barrier, inc=1, device_id={"ctx": across}, device_id_type=MESH)
    for k in range(1, outer):
        pl.semaphore_signal(barrier, inc=1, device_id={"ctx": lax.rem(me + 2 * k, n)},
                            device_id_type=MESH)
        pl.semaphore_signal(barrier, inc=1, device_id={"ctx": lax.rem(across + 2 * k, n)},
                            device_id_type=MESH)
    for k in range(1, ranks):
        pl.semaphore_signal(barrier, inc=1, device_id={"tp": lax.rem(rank + k, ranks)},
                            device_id_type=MESH)
    pl.semaphore_wait(
        barrier, 2 + 1 + 2 * (outer - 1) + ranks - 1 + pieces - own.astype(jnp.int32))

    def piece_copy(p):
        return pltpu.make_async_remote_copy(
            src_ref=pieces_ref.at[p], dst_ref=mine_ref.at[me],
            send_sem=piece_send.at[p], recv_sem=piece_recv.at[me],
            device_id={"ctx": rank * pieces + p}, device_id_type=MESH)

    own_piece = lax.max(me - rank * pieces, 0)
    local = pltpu.make_async_copy(
        pieces_ref.at[lax.min(own_piece, pieces - 1)], mine_ref.at[me], local_sem)

    for p in range(pieces):
        @pl.when(rank * pieces + p != me)
        def _():
            piece_copy(p).start()

    @pl.when(own)
    def _():
        local.start()

    def mine_copy(k):
        return pltpu.make_async_remote_copy(
            src_ref=mine_ref, dst_ref=mine_ref,
            send_sem=mine_send.at[k], recv_sem=mine_recv,
            device_id={"tp": lax.rem(rank + k, ranks)}, device_id_type=MESH)

    mask = (lax.broadcasted_iota(jnp.int32, (width, width), 0) // head
            == lax.broadcasted_iota(jnp.int32, (width, width), 1) // head)

    def spread(rows):
        return right_terms(jnp.where(mask, jnp.concatenate([rows] * tile, axis=0), 0.0))

    for g in range(groups):
        weights[g] = spread(weights_ref[:, g * width:(g + 1) * width])

    states_view = states_ref.reshape(CHUNKS, length, units)
    cot_view = cot_ref.reshape(CHUNKS, length, units)
    full_view = full.reshape(CHUNKS, length, units)
    blank = jnp.zeros((PAD - CHUNKS, units), F32)

    def token_rows(ref, t):
        return jnp.concatenate([ref[k, pl.ds(t, 1), :] for k in range(CHUNKS)] + [blank], axis=0)

    def slopes_at(t):
        h = token_rows(states_view, t)
        return 1.0 - h * h

    s_last = slopes_at(last)
    maps[last, rows_all:, :] = s_last * token_rows(cot_view, last)
    for k in range(CHUNKS):
        maps[last, k * head:(k + 1) * head, :] = weights_ref[...] * s_last[k:k + 1, :]

    def step(i, carry):
        t = last - 1 - i
        s = slopes_at(t)
        c = token_rows(cot_view, t)
        for g in range(groups):
            lanes = slice(g * width, (g + 1) * width)
            y = dot(left_terms(maps[t + 1, :, lanes]), weights[g])
            for k in range(CHUNKS):
                rows = slice(k * head, (k + 1) * head)
                maps[t, rows, lanes] = y[rows] * s[k:k + 1, lanes]
            maps[t, rows_all:, lanes] = s[:, lanes] * (c[:, lanes] + y[rows_all:])
        return carry

    lax.fori_loop(0, last, step, 0)

    @pl.when(own)
    def _():
        local.wait()
        for k in range(1, n):
            c = lax.rem(me + k, n)
            pltpu.make_async_remote_copy(
                src_ref=pieces_ref.at[0], dst_ref=mine_ref.at[c],
                send_sem=piece_send.at[0], recv_sem=piece_recv.at[c],
                device_id={"ctx": c}, device_id_type=MESH).wait_recv()
        for k in range(1, ranks):
            mine_copy(k).start()

    state = [None] * groups
    for k in range(CHUNKS - 1, -1, -1):
        rows = slice(k * head, (k + 1) * head)
        for g in range(groups):
            lanes = slice(g * width, (g + 1) * width)
            vec = maps[0, rows_all + k:rows_all + k + 1, lanes]
            if k == CHUNKS - 1:
                running = maps[0, rows, lanes]
            else:
                y = dot(left_terms(state[g]), spread(maps[0, rows, lanes]))
                running = y[:head]
                vec = vec + y[head:head + 1]
            state[g] = jnp.concatenate([running, jnp.broadcast_to(vec, (PAD, width))], axis=0)
            suffix[rows, lanes] = running
            suffix_vec[k:k + 1, lanes] = vec

    ones = mask.astype(F32).astype(BF16)
    ones2 = jnp.concatenate([ones, ones], axis=0)
    pick = (lax.broadcasted_iota(jnp.int32, (head, width), 1) % head
            == lax.broadcasted_iota(jnp.int32, (head, width), 0))

    def marked(row):
        high, low = halves(jnp.where(pick, jnp.broadcast_to(row, (head, width)), 0.0))
        return jnp.concatenate([high, low], axis=1)

    for g in range(groups):
        relay_weights[g] = spread(suffix[0:head, g * width:(g + 1) * width])

    copy = pltpu.make_async_remote_copy(
        src_ref=e_out, dst_ref=e_in, send_sem=send_sem, recv_sem=recv_sem,
        device_id={"ctx": lax.max(me - 1, 0)}, device_id_type=MESH)

    @pl.when(me == n - 1)
    def _():
        e_in[...] = jnp.zeros_like(e_in)

    @pl.when(me < n - 1)
    def _():
        copy.wait_recv()

    for g in range(groups):
        lanes = slice(g * width, (g + 1) * width)
        e = jnp.broadcast_to(e_in[:, lanes], (PAD, width))
        e_out[:, lanes] = suffix_vec[0:1, lanes] + dot(left_terms(e), relay_weights[g])[0:1]

    @pl.when(me > 0)
    def _():
        copy.start()

    for g in range(groups):
        lanes = slice(g * width, (g + 1) * width)
        e = dot(marked(e_in[:, lanes]), ones2)
        starts = [marked(suffix_vec[k:k + 1, lanes] + jnp.sum(
            e * suffix[k * head:(k + 1) * head, lanes], axis=0, keepdims=True))
            for k in range(1, CHUNKS)]
        spread_e[:rows_all - head, lanes] = dot(jnp.concatenate(starts, axis=0), ones2)
        spread_e[rows_all - head:, lanes] = e

    def line_copy(g, o):
        return pltpu.make_async_remote_copy(
            src_ref=blocks.at[me, g], dst_ref=blocks.at[me, g],
            send_sem=line_send.at[g, o], recv_sem=block_recv.at[me, g],
            device_id={"ctx": 2 * o + lax.rem(me, 2)}, device_id_type=MESH)

    def far_copy(g, o):
        return pltpu.make_async_remote_copy(
            src_ref=blocks.at[me, g], dst_ref=blocks.at[me, g],
            send_sem=far_send.at[g, o], recv_sem=block_recv.at[me, g],
            device_id={"ctx": 2 * o + 1 - lax.rem(me, 2)}, device_id_type=MESH)

    def pair_copy(g, o):
        c = 2 * o + lax.rem(me, 2)
        return pltpu.make_async_remote_copy(
            src_ref=blocks.at[c, g], dst_ref=blocks.at[c, g],
            send_sem=pair_send.at[g, o], recv_sem=block_recv.at[c, g],
            device_id={"ctx": across}, device_id_type=MESH)

    def arrived(c, g):
        pltpu.make_async_remote_copy(
            src_ref=blocks.at[c, g], dst_ref=blocks.at[c, g],
            send_sem=line_send.at[g, 0], recv_sem=block_recv.at[c, g],
            device_id={"ctx": across}, device_id_type=MESH).wait_recv()

    place = me // 2
    for g in range(groups):
        lanes = slice(g * width, (g + 1) * width)
        for k in range(CHUNKS):
            rows = slice(k * head, (k + 1) * head)
            e = spread_e[rows, lanes]

            def solve(t, carry):
                value = maps[t, rows_all + k:rows_all + k + 1, lanes] + jnp.sum(
                    maps[t, rows, lanes] * e, axis=0, keepdims=True)
                full_view[k, pl.ds(t, 1), lanes] = value
                return carry

            lax.fori_loop(0, length, solve, 0, unroll=8)
        blocks[me, g] = full[:, lanes].astype(BF16)
        pair_copy(g, place).start()

        def send(o, carry):
            @pl.when(o != place)
            def _():
                line_copy(g, o).start()

            @pl.when(o < place)
            def _():
                far_copy(g, o).start()
            return carry

        lax.fori_loop(0, outer, send, 0)

    @pl.when(jnp.logical_not(own))
    def _():
        mine_copy(1).wait_recv()

    total[...] = jnp.zeros_like(total)

    def gather(i, carry):
        o = outer - 1 - i
        near = 2 * o + lax.rem(me, 2)

        @pl.when(o != place)
        def _():
            for g in range(groups):
                arrived(near, g)

                @pl.when(o < place)
                def _():
                    pair_copy(g, o).start()

        for g in range(groups):
            total[:, g * width:(g + 1) * width] += dot(mine_ref[near], blocks[near, g])
        return carry

    lax.fori_loop(0, outer, gather, 0)

    share = total.shape[0] // ranks

    def rows_copy(t, source, g):
        start = pl.multiple_of(source * units + g * width, 128)
        return pltpu.make_async_remote_copy(
            src_ref=total.at[pl.ds(t * share, share), pl.ds(g * width, width)],
            dst_ref=out_ref.at[:, pl.ds(start, width)],
            send_sem=rows_send.at[g, t], recv_sem=rows_recv.at[g, source],
            device_id={"tp": t}, device_id_type=MESH)

    for g in range(groups):
        lanes = slice(g * width, (g + 1) * width)

        def collect(i, carry):
            far = 2 * (outer - 1 - i) + 1 - lax.rem(me, 2)
            arrived(far, g)
            total[:, lanes] += dot(mine_ref[far], blocks[far, g])
            return carry

        lax.fori_loop(0, outer, collect, 0)
        for k in range(1, ranks):
            rows_copy(lax.rem(rank + k, ranks), rank, g).start()
        out_ref[:, pl.ds(pl.multiple_of(rank * units + g * width, 128), width)] = total[
            pl.ds(pl.multiple_of(rank * share, 8), share), lanes]

    @pl.when(me > 0)
    def _():
        copy.wait_send()

    for p in range(pieces):
        @pl.when(rank * pieces + p != me)
        def _():
            piece_copy(p).wait_send()

    @pl.when(own)
    def _():
        for k in range(1, ranks):
            mine_copy(k).wait_send()

    def drain(o, carry):
        for g in range(groups):
            @pl.when(o <= place)
            def _():
                pair_copy(g, o).wait_send()

            @pl.when(o < place)
            def _():
                far_copy(g, o).wait_send()

            @pl.when(o != place)
            def _():
                line_copy(g, o).wait_send()
        return carry

    lax.fori_loop(0, outer, drain, 0)
    for k in range(1, ranks):
        t = lax.rem(rank + k, ranks)
        for g in range(groups):
            rows_copy(t, t, g).wait_recv()
            rows_copy(t, rank, g).wait_send()


def on_device(layer_inputs, states, cotangent, block_weights):
    tokens, units = states.shape
    heads, head, _ = block_weights.shape
    n = lax.axis_size("ctx")
    ranks = lax.axis_size("tp")
    features = layer_inputs.shape[1]
    columns = features * ranks // n
    pieces = features // columns
    length = tokens // CHUNKS
    width = min(256, units)
    flat = jnp.transpose(block_weights, (1, 0, 2)).reshape(head, units)
    cut = jnp.transpose(layer_inputs).reshape(pieces, columns, tokens)
    groups = units // width
    vmem = pl.BlockSpec(memory_space=pltpu.VMEM)
    return pl.pallas_call(
        backward,
        out_shape=jax.ShapeDtypeStruct((columns // ranks, units * ranks), F32),
        in_specs=[vmem] * 4,
        out_specs=vmem,
        scratch_shapes=[
            pltpu.VMEM((length, CHUNKS * head + PAD, units), F32),
            pltpu.VMEM((groups, 3 * width, width), BF16),
            pltpu.VMEM((groups, 3 * width, width), BF16),
            pltpu.VMEM((CHUNKS * head, units), F32),
            pltpu.VMEM((CHUNKS, units), F32),
            pltpu.VMEM((CHUNKS * head, units), F32),
            pltpu.VMEM((tokens, units), F32),
            pltpu.VMEM((n, columns, tokens), BF16),
            pltpu.VMEM((n, groups, tokens, width), BF16),
            pltpu.VMEM((columns, units), F32),
            pltpu.VMEM((1, units), F32),
            pltpu.VMEM((1, units), F32),
            pltpu.SemaphoreType.DMA,
            pltpu.SemaphoreType.DMA,
            pltpu.SemaphoreType.DMA,
            pltpu.SemaphoreType.DMA((pieces,)),
            pltpu.SemaphoreType.DMA((n,)),
            pltpu.SemaphoreType.DMA((ranks,)),
            pltpu.SemaphoreType.DMA,
            pltpu.SemaphoreType.DMA((groups, n // 2)),
            pltpu.SemaphoreType.DMA((groups, n // 2)),
            pltpu.SemaphoreType.DMA((groups, n // 2)),
            pltpu.SemaphoreType.DMA((n, groups)),
            pltpu.SemaphoreType.DMA((groups, ranks)),
            pltpu.SemaphoreType.DMA((groups, ranks)),
        ],
        compiler_params=pltpu.CompilerParams(
            collective_id=0, has_side_effects=True, vmem_limit_bytes=48 * 1024 * 1024),
    )(states, cotangent, flat, cut)


def solution(mesh):
    in_specs = (P("ctx", "tp"), P("ctx", "tp"), P("ctx", "tp"), P("tp", None, None))
    out_specs = P(("ctx", "tp"), None)
    return jax.shard_map(
        on_device, mesh=mesh, in_specs=in_specs, out_specs=out_specs, check_vma=False
    )
```

```python
import jax
import jax.numpy as jnp
from jax import lax
from jax.experimental import pallas as pl
from jax.experimental.pallas import tpu as pltpu
from jax.sharding import PartitionSpec as P

MESH = pl.DeviceIdType.MESH
CHUNKS = 8
PAD = 16
F32 = jnp.float32
BF16 = jnp.bfloat16


def halves(value):
    high = value.astype(BF16)
    low = (value - high.astype(F32)).astype(BF16)
    return high, low


def dot(left, right):
    return jnp.dot(left, right, preferred_element_type=F32)


def left_terms(value):
    high, low = halves(value)
    return jnp.concatenate([high, low, high], axis=1)


def right_terms(value):
    high, low = halves(value)
    return jnp.concatenate([high, high, low], axis=0)


def backward(states_ref, cot_ref, weights_ref, pieces_ref, out_ref,
             maps, weights, relay_weights, suffix, suffix_vec, spread_e, full, mine_ref, blocks,
             total, e_in, e_out, send_sem, recv_sem, local_sem, piece_send, piece_recv,
             mine_send, mine_recv, line_send, pair_send, block_recv, rows_send, rows_recv):
    n = lax.axis_size("ctx")
    ranks = lax.axis_size("tp")
    me = lax.axis_index("ctx")
    rank = lax.axis_index("tp")
    tokens, units = states_ref.shape
    head = weights_ref.shape[0]
    length = tokens // CHUNKS
    width = min(256, units)
    groups = units // width
    tile = width // head
    rows_all = CHUNKS * head
    pieces = pieces_ref.shape[0]
    last = length - 1
    outer = n // 2

    barrier = pltpu.get_barrier_semaphore()
    pl.semaphore_signal(barrier, inc=1, device_id={"ctx": lax.rem(me + 1, n)}, device_id_type=MESH)
    pl.semaphore_signal(barrier, inc=1, device_id={"ctx": lax.rem(me + n - 1, n)}, device_id_type=MESH)
    own = me // pieces == rank

    @pl.when(own)
    def _():
        for k in range(1, n):
            pl.semaphore_signal(barrier, inc=1, device_id={"ctx": lax.rem(me + k, n)},
                                device_id_type=MESH)
    across = me + 1 - 2 * lax.rem(me, 2)
    pl.semaphore_signal(barrier, inc=1, device_id={"ctx": across}, device_id_type=MESH)
    for k in range(1, outer):
        pl.semaphore_signal(barrier, inc=1, device_id={"ctx": lax.rem(me + 2 * k, n)},
                            device_id_type=MESH)
    for k in range(1, ranks):
        pl.semaphore_signal(barrier, inc=1, device_id={"tp": lax.rem(rank + k, ranks)},
                            device_id_type=MESH)
    pl.semaphore_wait(
        barrier, 2 + 1 + outer - 1 + ranks - 1 + pieces - own.astype(jnp.int32))

    def piece_copy(p):
        return pltpu.make_async_remote_copy(
            src_ref=pieces_ref.at[p], dst_ref=mine_ref.at[me],
            send_sem=piece_send.at[p], recv_sem=piece_recv.at[me],
            device_id={"ctx": rank * pieces + p}, device_id_type=MESH)

    own_piece = lax.max(me - rank * pieces, 0)
    local = pltpu.make_async_copy(
        pieces_ref.at[lax.min(own_piece, pieces - 1)], mine_ref.at[me], local_sem)

    for p in range(pieces):
        @pl.when(rank * pieces + p != me)
        def _():
            piece_copy(p).start()

    @pl.when(own)
    def _():
        local.start()

    def mine_copy(k):
        return pltpu.make_async_remote_copy(
            src_ref=mine_ref, dst_ref=mine_ref,
            send_sem=mine_send.at[k], recv_sem=mine_recv,
            device_id={"tp": lax.rem(rank + k, ranks)}, device_id_type=MESH)

    mask = (lax.broadcasted_iota(jnp.int32, (width, width), 0) // head
            == lax.broadcasted_iota(jnp.int32, (width, width), 1) // head)

    def spread(rows):
        return right_terms(jnp.where(mask, jnp.concatenate([rows] * tile, axis=0), 0.0))

    for g in range(groups):
        weights[g] = spread(weights_ref[:, g * width:(g + 1) * width])

    states_view = states_ref.reshape(CHUNKS, length, units)
    cot_view = cot_ref.reshape(CHUNKS, length, units)
    full_view = full.reshape(CHUNKS, length, units)
    blank = jnp.zeros((PAD - CHUNKS, units), F32)

    def token_rows(ref, t):
        return jnp.concatenate([ref[k, pl.ds(t, 1), :] for k in range(CHUNKS)] + [blank], axis=0)

    def slopes_at(t):
        h = token_rows(states_view, t)
        return 1.0 - h * h

    s_last = slopes_at(last)
    maps[last, rows_all:, :] = s_last * token_rows(cot_view, last)
    for k in range(CHUNKS):
        maps[last, k * head:(k + 1) * head, :] = weights_ref[...] * s_last[k:k + 1, :]

    def step(i, carry):
        t = last - 1 - i
        s = slopes_at(t)
        c = token_rows(cot_view, t)
        for g in range(groups):
            lanes = slice(g * width, (g + 1) * width)
            y = dot(left_terms(maps[t + 1, :, lanes]), weights[g])
            for k in range(CHUNKS):
                rows = slice(k * head, (k + 1) * head)
                maps[t, rows, lanes] = y[rows] * s[k:k + 1, lanes]
            maps[t, rows_all:, lanes] = s[:, lanes] * (c[:, lanes] + y[rows_all:])
        return carry

    lax.fori_loop(0, last, step, 0)

    @pl.when(own)
    def _():
        local.wait()
        for k in range(1, n):
            c = lax.rem(me + k, n)
            pltpu.make_async_remote_copy(
                src_ref=pieces_ref.at[0], dst_ref=mine_ref.at[c],
                send_sem=piece_send.at[0], recv_sem=piece_recv.at[c],
                device_id={"ctx": c}, device_id_type=MESH).wait_recv()
        for k in range(1, ranks):
            mine_copy(k).start()

    state = [None] * groups
    for k in range(CHUNKS - 1, -1, -1):
        rows = slice(k * head, (k + 1) * head)
        for g in range(groups):
            lanes = slice(g * width, (g + 1) * width)
            vec = maps[0, rows_all + k:rows_all + k + 1, lanes]
            if k == CHUNKS - 1:
                running = maps[0, rows, lanes]
            else:
                y = dot(left_terms(state[g]), spread(maps[0, rows, lanes]))
                running = y[:head]
                vec = vec + y[head:head + 1]
            state[g] = jnp.concatenate([running, jnp.broadcast_to(vec, (PAD, width))], axis=0)
            suffix[rows, lanes] = running
            suffix_vec[k:k + 1, lanes] = vec

    ones = mask.astype(F32).astype(BF16)
    ones2 = jnp.concatenate([ones, ones], axis=0)
    pick = (lax.broadcasted_iota(jnp.int32, (head, width), 1) % head
            == lax.broadcasted_iota(jnp.int32, (head, width), 0))

    def marked(row):
        high, low = halves(jnp.where(pick, jnp.broadcast_to(row, (head, width)), 0.0))
        return jnp.concatenate([high, low], axis=1)

    for g in range(groups):
        relay_weights[g] = spread(suffix[0:head, g * width:(g + 1) * width])

    copy = pltpu.make_async_remote_copy(
        src_ref=e_out, dst_ref=e_in, send_sem=send_sem, recv_sem=recv_sem,
        device_id={"ctx": lax.max(me - 1, 0)}, device_id_type=MESH)

    @pl.when(me == n - 1)
    def _():
        e_in[...] = jnp.zeros_like(e_in)

    @pl.when(me < n - 1)
    def _():
        copy.wait_recv()

    for g in range(groups):
        lanes = slice(g * width, (g + 1) * width)
        e = jnp.broadcast_to(e_in[:, lanes], (PAD, width))
        e_out[:, lanes] = suffix_vec[0:1, lanes] + dot(left_terms(e), relay_weights[g])[0:1]

    @pl.when(me > 0)
    def _():
        copy.start()

    for g in range(groups):
        lanes = slice(g * width, (g + 1) * width)
        e = dot(marked(e_in[:, lanes]), ones2)
        starts = [marked(suffix_vec[k:k + 1, lanes] + jnp.sum(
            e * suffix[k * head:(k + 1) * head, lanes], axis=0, keepdims=True))
            for k in range(1, CHUNKS)]
        spread_e[:rows_all - head, lanes] = dot(jnp.concatenate(starts, axis=0), ones2)
        spread_e[rows_all - head:, lanes] = e

    def line_copy(g, o):
        return pltpu.make_async_remote_copy(
            src_ref=blocks.at[me, g], dst_ref=blocks.at[me, g],
            send_sem=line_send.at[g, o], recv_sem=block_recv.at[me, g],
            device_id={"ctx": 2 * o + lax.rem(me, 2)}, device_id_type=MESH)

    def pair_copy(g, o):
        c = 2 * o + lax.rem(me, 2)
        return pltpu.make_async_remote_copy(
            src_ref=blocks.at[c, g], dst_ref=blocks.at[c, g],
            send_sem=pair_send.at[g, o], recv_sem=block_recv.at[c, g],
            device_id={"ctx": across}, device_id_type=MESH)

    def arrived(c, g):
        pltpu.make_async_remote_copy(
            src_ref=blocks.at[c, g], dst_ref=blocks.at[c, g],
            send_sem=line_send.at[g, 0], recv_sem=block_recv.at[c, g],
            device_id={"ctx": across}, device_id_type=MESH).wait_recv()

    place = me // 2
    for g in range(groups):
        lanes = slice(g * width, (g + 1) * width)
        for k in range(CHUNKS):
            rows = slice(k * head, (k + 1) * head)
            e = spread_e[rows, lanes]

            def solve(t, carry):
                value = maps[t, rows_all + k:rows_all + k + 1, lanes] + jnp.sum(
                    maps[t, rows, lanes] * e, axis=0, keepdims=True)
                full_view[k, pl.ds(t, 1), lanes] = value
                return carry

            lax.fori_loop(0, length, solve, 0, unroll=8)
        blocks[me, g] = full[:, lanes].astype(BF16)
        pair_copy(g, place).start()

        def send(o, carry):
            @pl.when(o != place)
            def _():
                line_copy(g, o).start()
            return carry

        lax.fori_loop(0, outer, send, 0)

    total[...] = jnp.zeros_like(total)

    def gather(i, carry):
        o = outer - 1 - i
        near = 2 * o + lax.rem(me, 2)

        @pl.when(o != place)
        def _():
            for g in range(groups):
                arrived(near, g)
                pair_copy(g, o).start()

        return carry

    lax.fori_loop(0, outer, gather, 0)

    @pl.when(jnp.logical_not(own))
    def _():
        mine_copy(1).wait_recv()

    def multiply(i, carry):
        near = 2 * (outer - 1 - i) + lax.rem(me, 2)
        for g in range(groups):
            total[:, g * width:(g + 1) * width] += dot(mine_ref[near], blocks[near, g])
        return carry

    lax.fori_loop(0, outer, multiply, 0)

    share = total.shape[0] // ranks

    def rows_copy(t, source, g):
        start = pl.multiple_of(source * units + g * width, 128)
        return pltpu.make_async_remote_copy(
            src_ref=total.at[pl.ds(t * share, share), pl.ds(g * width, width)],
            dst_ref=out_ref.at[:, pl.ds(start, width)],
            send_sem=rows_send.at[g, t], recv_sem=rows_recv.at[g, source],
            device_id={"tp": t}, device_id_type=MESH)

    for g in range(groups):
        lanes = slice(g * width, (g + 1) * width)

        def collect(i, carry):
            far = 2 * (outer - 1 - i) + 1 - lax.rem(me, 2)
            arrived(far, g)
            total[:, lanes] += dot(mine_ref[far], blocks[far, g])
            return carry

        lax.fori_loop(0, outer, collect, 0)
        for k in range(1, ranks):
            rows_copy(lax.rem(rank + k, ranks), rank, g).start()
        out_ref[:, pl.ds(pl.multiple_of(rank * units + g * width, 128), width)] = total[
            pl.ds(pl.multiple_of(rank * share, 8), share), lanes]

    @pl.when(me > 0)
    def _():
        copy.wait_send()

    for p in range(pieces):
        @pl.when(rank * pieces + p != me)
        def _():
            piece_copy(p).wait_send()

    @pl.when(own)
    def _():
        for k in range(1, ranks):
            mine_copy(k).wait_send()

    def drain(o, carry):
        for g in range(groups):
            pair_copy(g, o).wait_send()

            @pl.when(o != place)
            def _():
                line_copy(g, o).wait_send()
        return carry

    lax.fori_loop(0, outer, drain, 0)
    for k in range(1, ranks):
        t = lax.rem(rank + k, ranks)
        for g in range(groups):
            rows_copy(t, t, g).wait_recv()
            rows_copy(t, rank, g).wait_send()


def on_device(layer_inputs, states, cotangent, block_weights):
    tokens, units = states.shape
    heads, head, _ = block_weights.shape
    n = lax.axis_size("ctx")
    ranks = lax.axis_size("tp")
    features = layer_inputs.shape[1]
    columns = features * ranks // n
    pieces = features // columns
    length = tokens // CHUNKS
    width = min(256, units)
    flat = jnp.transpose(block_weights, (1, 0, 2)).reshape(head, units)
    cut = jnp.transpose(layer_inputs).reshape(pieces, columns, tokens)
    groups = units // width
    vmem = pl.BlockSpec(memory_space=pltpu.VMEM)
    return pl.pallas_call(
        backward,
        out_shape=jax.ShapeDtypeStruct((columns // ranks, units * ranks), F32),
        in_specs=[vmem] * 4,
        out_specs=vmem,
        scratch_shapes=[
            pltpu.VMEM((length, CHUNKS * head + PAD, units), F32),
            pltpu.VMEM((groups, 3 * width, width), BF16),
            pltpu.VMEM((groups, 3 * width, width), BF16),
            pltpu.VMEM((CHUNKS * head, units), F32),
            pltpu.VMEM((CHUNKS, units), F32),
            pltpu.VMEM((CHUNKS * head, units), F32),
            pltpu.VMEM((tokens, units), F32),
            pltpu.VMEM((n, columns, tokens), BF16),
            pltpu.VMEM((n, groups, tokens, width), BF16),
            pltpu.VMEM((columns, units), F32),
            pltpu.VMEM((1, units), F32),
            pltpu.VMEM((1, units), F32),
            pltpu.SemaphoreType.DMA,
            pltpu.SemaphoreType.DMA,
            pltpu.SemaphoreType.DMA,
            pltpu.SemaphoreType.DMA((pieces,)),
            pltpu.SemaphoreType.DMA((n,)),
            pltpu.SemaphoreType.DMA((ranks,)),
            pltpu.SemaphoreType.DMA,
            pltpu.SemaphoreType.DMA((groups, n // 2)),
            pltpu.SemaphoreType.DMA((groups, n // 2)),
            pltpu.SemaphoreType.DMA((n, groups)),
            pltpu.SemaphoreType.DMA((groups, ranks)),
            pltpu.SemaphoreType.DMA((groups, ranks)),
        ],
        compiler_params=pltpu.CompilerParams(
            collective_id=0, has_side_effects=True, vmem_limit_bytes=48 * 1024 * 1024),
    )(states, cotangent, flat, cut)


def solution(mesh):
    in_specs = (P("ctx", "tp"), P("ctx", "tp"), P("ctx", "tp"), P("tp", None, None))
    out_specs = P(("ctx", "tp"), None)
    return jax.shard_map(
        on_device, mesh=mesh, in_specs=in_specs, out_specs=out_specs, check_vma=False
    )
```
